32 devices in a mesh: grp: 4 (over z), dev: 8 (over y, x, core).
Axes of the slice: x: 2, y: 2, z: 4, core: 2. Of those that a mesh axis runs over, the one named last changes fastest.
Arguments:
- omega: float32 [4, 32, 256, 128], P('grp', 'dev'), may hold values from -6 to 6
- u_factor: float32 [4, 32, 80, 256, 32], P('grp', 'dev'), may hold values from -0.0625 to 0.0625
- v_factor: float32 [4, 32, 80, 256, 32], P('grp', 'dev'), may hold values from -0.375 to 0.375
- columns: int32 [4, 32, 80, 1], P('grp', 'dev'), may hold values from 0 to 31; in each aligned block of 320 rows (0 to 319, 320 to 639, ..., all dimensions but the last counted through in order) at most 11 rows name the same one
- ranks: int32 [4, 32, 80], P('grp', 'dev'), may hold values from 8 to 32
Outputs:
- leaf_basis: float32 [32, 256, 128], P('dev', 'grp')
- transfer: float32 [32, 256, 128], P('dev')
The draws below stay inside these ranges and needn't reach their ends.
Inputs may be any that keep to these rules, and one draw needn't show every extreme that they name: `columns`: within the 320 blocks of one device's row clusters in one group, at most 11 name any one column cluster, and some column cluster is named by exactly 11.
All inputs are finite; a program needn't handle non-finite values.
Results may differ from the reference program's by a relative error of at most 0.0003.
Values sent between devices are 32-bit elements; how exact they have to be, the bound alone decides.
No kernel may reach another device: no remote copies, remote signals or barrier semaphores. Data moves between devices by JAX's collectives and lax.ppermute only.
A program may use at most 192 MiB of HBM per device.

```python
import math
import jax
import jax.numpy as jnp
import numpy as np
from jax import lax

CL = 4
NB = 80
LEAF = 256
K = 32
P_SIZE = 128
CLUSTERS = 32
MOSTC = 11
N_GRP = 4
N_DEV = 8


def plant(values, key, smallest, top_value):
    longest = values.shape.index(max(values.shape))
    spots = []
    for shift in (0, 1):
        where = [jax.random.randint(jax.random.fold_in(key, axis), (), 0, length) for axis, length in enumerate(values.shape)]
        where[longest] = (where[longest] + shift) % values.shape[longest]
        spots.append(tuple(where))
    return values.at[spots[0]].set(smallest).at[spots[1]].set(top_value)


def shard_levels(key, dims, cuts, smallest, top_value):
    def one(position, blocks):
        steps = jax.random.uniform(jax.random.fold_in(jax.random.fold_in(key, 6), position), (blocks,), jnp.float32, smallest / len(cuts), top_value / len(cuts))
        return jnp.repeat(jnp.exp(steps), dims[position] // blocks).reshape((-1,) + (1,) * (len(dims) - position - 1))

    gain = one(*cuts[0])
    for cut in cuts[1:]:
        gain = gain * one(*cut)
    return gain


def deal_out(stream_key, own, number, rows, count, top, most, slope):
    ranking = jax.random.permutation(stream_key, count)
    packed, ordinary = portions_of(count, rows * top, most, slope, True), portions_of(count, rows * top, most, slope, False)
    places = jnp.arange(count)

    def named(lengths, turn):
        used = int((lengths > 0).sum())
        fixed = max(1, used // 4)
        moved = fixed + (places - fixed + turn * (used - fixed)) % max(1, count - fixed)
        return jnp.zeros((count,), jnp.int32).at[ranking[jnp.where(places < fixed, places, moved)]].set(jnp.asarray(lengths, jnp.int32))

    lengths = jnp.where(number % 4 == 0, named(packed, number // 4), named(ordinary, number - number // 4 - 1))
    mixed = jax.random.permutation(jax.random.fold_in(own, 3), count)
    giver, receiver = mixed[0:count // 2 * 2:2], mixed[1:count // 2 * 2:2]
    slack = jnp.minimum(lengths[giver] - 1, most - lengths[receiver]) // 2
    slack = jnp.where((giver == ranking[0]) | (receiver == ranking[0]) | (lengths[receiver] == 0), 0, jnp.maximum(slack, 0))
    moved = jax.random.randint(jax.random.fold_in(own, 4), (count // 2,), 0, 1 << 20) % (slack + 1)
    lengths = lengths.at[giver].add(-moved).at[receiver].add(moved)
    items = jnp.searchsorted(jnp.cumsum(lengths), jnp.arange(rows * top), side="right").astype(jnp.int32)
    table = items.reshape(top, rows).T
    table = table[jax.random.permutation(jax.random.fold_in(own, 1), rows)]
    turn = jax.random.randint(jax.random.fold_in(own, 2), (rows, 1), 0, top)
    return jnp.take_along_axis(table, (jnp.arange(top)[None, :] + turn) % top, axis=1)


def portions_of(count, total, bound, lean, full):
    portions = [(1 << 20) // math.isqrt(grade ** lean) + 1 for grade in range(1, count + 1)]
    largest = bound if full else min(bound, max(-(-total // count), total * portions[0] // sum(portions)))
    least = 1 if total - largest >= count - 1 else 0
    counts, rest = [largest] + [least] * (count - 1), total - largest - least * (count - 1)
    while rest > 0:
        candidates = [i for i in range(1, count) if counts[i] < largest] or [i for i in range(1, count) if counts[i] < bound]
        pool, left = sum([portions[i] for i in candidates]), rest
        for i in candidates:
            addition = min(bound - counts[i], max(1, left * portions[i] // pool), rest)
            counts[i] = counts[i] + addition
            rest = rest - addition
    return np.array(counts)


def centred(own_key, shape, width, most, cuts=(), held_as=jnp.bfloat16):
    values = width * jax.random.normal(own_key, shape, jnp.float32)
    if cuts:
        values = values * shard_levels(own_key, shape, cuts, -0.22, 0.18)
    return jnp.clip(values, -most, most).astype(held_as)


def setup_inputs(seed: int = 0) -> dict:
    arg_keys = jax.random.split(jax.random.key(seed), 6)
    omega = centred(arg_keys[0], (N_GRP, CLUSTERS, LEAF, P_SIZE), 1.0, 6.0, ((0, 4), (1, 8)), jnp.float32)
    u_factor = centred(arg_keys[1], (N_GRP, CLUSTERS, NB, LEAF, K), (N_GRP * NB * K) ** -0.5, 0.0625, ((0, 4), (1, 8)), jnp.float32)
    v_factor = centred(arg_keys[2], (N_GRP, CLUSTERS, NB, LEAF, K), LEAF ** -0.5, 0.375, ((0, 4), (1, 8)), jnp.float32)
    columns_keys = jax.random.split(jax.random.fold_in(arg_keys[3], 1), N_GRP * CLUSTERS * NB // (CL * NB))
    columns_turns = jax.random.permutation(jax.random.fold_in(arg_keys[3], 3), N_GRP * CLUSTERS * NB // (CL * NB))
    columns = jax.vmap(lambda own, number: deal_out(jax.random.fold_in(arg_keys[3], 2), own, number, CL * NB, CLUSTERS, 1, MOSTC, 2))(columns_keys, columns_turns).reshape((N_GRP, CLUSTERS, NB, 1))
    ranks = plant(jax.random.randint(arg_keys[4], (N_GRP, CLUSTERS, NB), K // 4, K + 1), jax.random.fold_in(arg_keys[4], 1), K // 4, K).astype(jnp.int32)
    return {"omega": omega, "u_factor": u_factor, "v_factor": v_factor, "columns": columns, "ranks": ranks}


precise = lax.Precision.HIGHEST

def tree_node(left_factor, right_factor):
    gram_matrix = jnp.einsum('kp,kq->pq', left_factor, left_factor, precision=precise) + jnp.einsum('kp,kq->pq', right_factor, right_factor, precision=precise)
    lower_factor = jnp.linalg.cholesky(gram_matrix)
    stacked_rows = jnp.concatenate([left_factor, right_factor], axis=0)
    node_transfer = lax.linalg.triangular_solve(lower_factor, stacked_rows, left_side=False, lower=True, transpose_a=True)
    return (node_transfer, lower_factor.T)

def reference(omega, u_factor, v_factor, columns, ranks):
    sketch = jnp.zeros((CLUSTERS, LEAF, P_SIZE), jnp.float32)
    rank_index = jnp.arange(K, dtype=jnp.int32)
    for group_index in range(N_GRP):
        group_probe = omega[group_index]

        def cluster_sketch(pieces):
            u_rows, v_rows, col_ids, rank_vals = pieces
            rank_mask = (rank_index[None, :] < rank_vals[:, None]).astype(jnp.float32)
            coeff = jnp.einsum('bik,bip->bkp', v_rows, group_probe[col_ids], precision=precise)
            return jnp.einsum('bik,bkp->ip', u_rows * rank_mask[:, None, :], coeff, precision=precise)
        sketch = sketch + lax.map(cluster_sketch, (u_factor[group_index], v_factor[group_index], columns[group_index, :, :, 0], ranks[group_index]))
    gram_matrix = jnp.einsum('cip,ciq->cpq', sketch, sketch, precision=precise)
    lower_factor = jnp.linalg.cholesky(gram_matrix)
    leaf_basis = lax.linalg.triangular_solve(lower_factor, sketch, left_side=False, lower=True, transpose_a=True)
    factors = jnp.swapaxes(lower_factor, 1, 2)
    levels_out = []
    while factors.shape[0] > 1:
        made, factors = jax.vmap(tree_node)(factors[0::2], factors[1::2])
        levels_out.append(made)
    tree_part = jnp.zeros((N_DEV, 2 * P_SIZE, P_SIZE), jnp.float32)
    for depth_step, made in enumerate(levels_out[2:]):
        places = jnp.arange(made.shape[0], dtype=jnp.int32) * 2 ** (depth_step + 1) + (2 ** depth_step - 1)
        tree_part = tree_part.at[places].set(made)
    transfer = jnp.stack([levels_out[0][0::2], levels_out[0][1::2], levels_out[1], tree_part], axis=1)
    return (leaf_basis, transfer.reshape(CLUSTERS, 2 * P_SIZE, P_SIZE))
```

```python
import functools

import jax
import jax.numpy as jnp
from jax import lax
from jax.experimental import pallas as pl
from jax.experimental.pallas import tpu as pltpu
from jax.sharding import PartitionSpec as P


f32 = jnp.float32
bf16 = jnp.bfloat16
VM = pl.BlockSpec(memory_space=pltpu.VMEM)
SM = pl.BlockSpec(memory_space=pltpu.SMEM)


def swapped(value, axis, mask):
    pairs = [(source, source ^ mask) for source in range(lax.axis_size(axis))]
    return lax.ppermute(value, axis, pairs)


def split(x):
    high = x.astype(bf16)
    low = (x - high.astype(f32)).astype(bf16)
    return high, low


def dot_full(x, y, dims):
    return lax.dot_general(
        x, y, (dims, ((), ())), precision=lax.Precision.HIGHEST, preferred_element_type=f32
    )


def table_kernel(order, unit, n_local, cols_ref, ranks_ref, slot_ref):
    n_leaf, _, n_blocks = cols_ref.shape
    depth, clusters = slot_ref.shape
    position = lax.broadcasted_iota(jnp.int32, (clusters, 1), 0)
    names = jnp.zeros((clusters, 1), jnp.int32)
    for at, cluster in enumerate(order):
        names = jnp.where(position == at, cluster, names)
    names = jnp.bitwise_xor(names, lax.axis_index("dev") * n_local)
    ones = jnp.ones((n_blocks, n_blocks), bf16)
    si = lax.broadcasted_iota(jnp.int32, (n_blocks, n_blocks), 0)
    li = lax.broadcasted_iota(jnp.int32, (n_blocks, n_blocks), 1)
    before = jnp.where(si < li, 1.0, 0.0).astype(bf16)
    number = lax.broadcasted_iota(jnp.int32, (depth, n_blocks), 1).astype(f32)
    level = lax.broadcasted_iota(jnp.int32, (depth, n_blocks), 0).astype(f32)
    offset = jnp.zeros((clusters, n_blocks), f32)
    index = jnp.zeros((depth, clusters), f32)
    rank = jnp.zeros((depth, clusters), f32)
    used = jnp.zeros((depth, clusters), f32)
    for c in range(n_leaf):
        named = jnp.where(cols_ref[c] == names, 1.0, 0.0)
        named_low = named.astype(bf16)

        def listed(x, named_low=named_low):
            return lax.dot_general(
                x.astype(bf16), named_low, (((1,), (1,)), ((), ())), preferred_element_type=f32
            )

        ahead = offset + jnp.dot(named_low, before, preferred_element_type=f32)
        place = jnp.sum(named * ahead, axis=0, keepdims=True)
        mark = jnp.where(place == level, 1.0, 0.0)
        here = listed(mark)
        index = index + listed(mark * number) + here * float(c * n_blocks)
        rank = rank + listed(mark * ranks_ref[c : c + 1, :].astype(f32))
        used = used + here
        offset = offset + jnp.dot(named_low, ones, preferred_element_type=f32)
    index = jnp.where(used > 0.5, index, float(n_leaf * n_blocks))
    slot_ref[...] = index.astype(jnp.int32) * unit + rank.astype(jnp.int32)


def slot_table(order, cols, ranks, depth, unit, n_local):
    return pl.pallas_call(
        functools.partial(table_kernel, order, unit, n_local),
        out_shape=jax.ShapeDtypeStruct((depth, len(order)), jnp.int32),
        in_specs=[VM, VM],
        out_specs=VM,
        compiler_params=pltpu.CompilerParams(vmem_limit_bytes=4 << 20),
        cost_estimate=pl.CostEstimate(flops=0, bytes_accessed=24 << 20, transcendentals=0),
        name="slots",
    )(cols, ranks)


def coeff_kernel(most, start, unit, n_pieces, *refs):
    slot_ref, v_ref = refs[:2]
    pieces = refs[2 : 2 + n_pieces]
    c_ref, w_ref = refs[-2:]
    p = pieces[0].shape[2]
    n_all, k, _ = v_ref.shape
    at = 0
    for piece in pieces:
        for q in range(piece.shape[0]):
            high, low = split(piece[q])
            w_ref[at, :, :p] = high
            w_ref[at, :, p:] = low
            at += 1
    sub = lax.broadcasted_iota(jnp.int32, (k, p), 0)

    def body(j, _):
        highs, lows, ids, kept = [], [], [], []
        for n in range(most):
            entry = slot_ref[n, start + j]
            b = entry // unit
            ids.append(b)
            kept.append(sub < entry % unit)
            high, low = split(v_ref[jnp.minimum(b, n_all - 1)])
            highs.append(high)
            lows.append(low)
        w = w_ref[j]
        both = jnp.dot(jnp.concatenate(highs, 0), w, preferred_element_type=f32)
        both = both + jnp.dot(jnp.concatenate(lows, 0), w, preferred_element_type=f32)
        total = both[:, :p] + both[:, p:]
        for n in range(most):
            c_ref[ids[n]] = jnp.where(kept[n], total[n * k : (n + 1) * k], 0.0)
        return 0

    lax.fori_loop(0, at, body, 0, unroll=2)


def coefficients(slots, v, pieces, start, most, unit, before):
    n_all, k, rows = v.shape
    p = pieces[0].shape[2]
    held = sum(piece.shape[0] for piece in pieces)
    chained = before is not None
    args = [slots, v, *pieces] + ([before] if chained else [])
    return pl.pallas_call(
        functools.partial(coeff_kernel, most, start, unit, len(pieces)),
        out_shape=jax.ShapeDtypeStruct((n_all + 1, k, p), f32),
        in_specs=[SM, VM] + [VM] * len(pieces) + [VM] * chained,
        out_specs=VM,
        scratch_shapes=[pltpu.VMEM((held, rows, 2 * p), bf16)],
        input_output_aliases={len(args) - 1: 0} if chained else {},
        compiler_params=pltpu.CompilerParams(vmem_limit_bytes=8 << 20),
        cost_estimate=pl.CostEstimate(
            flops=held * most * k * rows * p * 8, bytes_accessed=8 << 20, transcendentals=0
        ),
        name="coeff",
    )(*args)


def sketch_kernel(m, n_blocks, c_ref, u_ref, o_ref):
    p, rows = o_ref.shape
    k = u_ref.shape[1]
    step = rows // k
    leaf = jnp.bitwise_xor(lax.axis_index("grp"), m)
    total = jnp.zeros((p, rows), f32)
    for q in range(n_blocks // step):
        at = pl.ds(leaf * n_blocks + q * step, step)
        high, low = split(c_ref[at].reshape(rows, p).T)
        u_high, u_low = split(u_ref[at].reshape(rows, rows))
        total = total + jnp.dot(high, u_high, preferred_element_type=f32)
        total = total + jnp.dot(low, u_high, preferred_element_type=f32)
        total = total + jnp.dot(high, u_low, preferred_element_type=f32)
    o_ref[...] = total


def sketch(coeff, u, m, n_blocks):
    k, rows = u.shape[1:]
    p = coeff.shape[2]
    return pl.pallas_call(
        functools.partial(sketch_kernel, m, n_blocks),
        out_shape=jax.ShapeDtypeStruct((p, rows), f32),
        in_specs=[VM, VM],
        out_specs=VM,
        compiler_params=pltpu.CompilerParams(vmem_limit_bytes=8 << 20),
        cost_estimate=pl.CostEstimate(
            flops=n_blocks * k * rows * p * 6, bytes_accessed=1 << 20, transcendentals=0
        ),
        name="sketch",
    )(coeff, u)


def gram_kernel(n_terms, *refs):
    terms = refs[:n_terms]
    near_ref, far_ref, keep_ref, hold_ref = refs[n_terms:]
    total = terms[0][...]
    for term in terms[1:]:
        total = total + term[...]
    gram = dot_full(total, total, ((1,), (1,)))
    hold_ref[...] = total.T
    p = gram.shape[0]
    quarter = keep_ref.shape[0]

    def rows_of(m):
        at = pl.multiple_of(jnp.bitwise_xor(lax.axis_index("grp"), m) * quarter, quarter)
        return hold_ref[pl.ds(at, quarter), :]

    keep_ref[...] = rows_of(0)
    near_ref[:quarter] = rows_of(1)
    near_ref[quarter : quarter + p] = gram
    near_ref[quarter + p :] = rows_of(3)
    far_ref[:p] = gram
    far_ref[p:] = rows_of(2)


def gram_of(terms, n_grp):
    p, rows = terms[0].shape
    quarter = rows // n_grp
    return pl.pallas_call(
        functools.partial(gram_kernel, len(terms)),
        out_shape=(
            jax.ShapeDtypeStruct((p + 2 * quarter, p), f32),
            jax.ShapeDtypeStruct((p + quarter, p), f32),
            jax.ShapeDtypeStruct((quarter, p), f32),
        ),
        in_specs=[VM] * len(terms),
        out_specs=(VM, VM, VM),
        scratch_shapes=[pltpu.VMEM((rows, p), f32)],
        compiler_params=pltpu.CompilerParams(vmem_limit_bytes=8 << 20),
        name="gram",
    )(*terms)


def tree_kernel(panel, n_leaf, n_levels, *refs):
    grams = refs[:n_leaf]
    rows_in = refs[n_leaf : 2 * n_leaf]
    lefts = refs[2 * n_leaf : 2 * n_leaf + n_levels]
    rights = refs[2 * n_leaf + n_levels : 2 * n_leaf + 2 * n_levels]
    basis_ref, tr_ref, m_ref = refs[2 * n_leaf + 2 * n_levels :]
    count, p, _ = m_ref.shape
    own = lax.axis_index("grp")
    device = lax.axis_index("dev")
    ri = lax.broadcasted_iota(jnp.int32, (p, p), 0)
    ci = lax.broadcasted_iota(jnp.int32, (p, p), 1)
    for m in range(n_leaf):
        m_ref[jnp.bitwise_xor(own, m)] = grams[m][...]
    identity = jnp.where(ri == ci, 1.0, 0.0)
    m_ref[7] = identity
    m_ref[8] = identity
    for level in range(n_levels):

        @pl.when(device % 2 ** (level + 1) == 2**level - 1)
        def _(level=level):
            m_ref[7] = lefts[level][...]
            m_ref[8] = rights[level][...]

    m_ref[4] = m_ref[0] + m_ref[1]
    m_ref[5] = m_ref[2] + m_ref[3]
    m_ref[6] = m_ref[4] + m_ref[5]
    m_ref[9] = m_ref[7] + m_ref[8]
    lane = lax.broadcasted_iota(jnp.int32, (1, 1, p), 2)
    sub8 = lax.broadcasted_iota(jnp.int32, (1, 8, p), 1)
    n_panels = p // panel
    n_tiles = panel // 8
    for pn in range(n_panels):
        base = pn * panel
        x = [m_ref[:, base + 8 * i : base + 8 * i + 8, :] for i in range(n_tiles)]
        for t in range(panel):
            i0, ts = t // 8, t % 8
            k = base + t
            columns = [jnp.broadcast_to(x[i][:, :, k : k + 1], x[i].shape) for i in range(i0, n_tiles)]
            scale = lax.rsqrt(columns[0][:, ts : ts + 1, :])
            hit = lane == k
            row = jnp.where(hit, 1.0, x[i0][:, ts : ts + 1, :]) * scale
            for i in range(i0, n_tiles):
                new = jnp.where(hit, 0.0, x[i]) - (columns[i - i0] * scale) * row
                if i == i0:
                    new = jnp.where(sub8 < ts, x[i], jnp.where(sub8 == ts, row, new))
                x[i] = new
        for i in range(n_tiles):
            m_ref[:, base + 8 * i : base + 8 * i + 8, :] = x[i]
        if pn < n_panels - 1:
            after = base + panel
            for b in range(count):
                block = m_ref[b, base:after, :]
                si = lax.broadcasted_iota(jnp.int32, block.shape, 0)
                li = lax.broadcasted_iota(jnp.int32, block.shape, 1)
                right = jnp.where((li < after) & (li - base > si), 0.0, block)
                change = dot_full(block.T[after:, :], right, ((1,), (0,)))
                old = m_ref[b, after:, :]
                lj = lax.broadcasted_iota(jnp.int32, old.shape, 1)
                old = jnp.where((lj >= base) & (lj < after), 0.0, old)
                m_ref[b, after:, :] = old - change

    def inverse(b):
        return jnp.where(ci <= ri, m_ref[b], 0.0)

    def upper(b):
        whole = m_ref[b]
        return jnp.where(ci > ri, whole, jnp.where(ci == ri, 1.0 / whole, 0.0))

    for m in range(n_leaf):
        leaf = jnp.bitwise_xor(own, m)
        basis_ref[leaf] = dot_full(rows_in[m][...], inverse(leaf), ((1,), (1,)))
    keep = device != lax.axis_size("dev") - 1
    for q, (a, b, node) in enumerate(((0, 1, 4), (2, 3, 5), (4, 5, 6), (7, 8, 9))):
        solve = inverse(node)
        top = dot_full(upper(a), solve, ((1,), (1,)))
        bottom = dot_full(upper(b), solve, ((1,), (1,)))
        if q == 3:
            top = jnp.where(keep, top, 0.0)
            bottom = jnp.where(keep, bottom, 0.0)
        tr_ref[q, :p] = top
        tr_ref[q, p:] = bottom


def tree(grams, rows_in, lefts, rights, panel=32):
    quarter, p = rows_in[0].shape
    n_leaf = len(grams)
    arrays = [*grams, *rows_in, *lefts, *rights]
    return pl.pallas_call(
        functools.partial(tree_kernel, panel, n_leaf, len(lefts)),
        out_shape=(
            jax.ShapeDtypeStruct((n_leaf, quarter, p), f32),
            jax.ShapeDtypeStruct((4, 2 * p, p), f32),
        ),
        in_specs=[VM] * len(arrays),
        out_specs=(VM, VM),
        scratch_shapes=[pltpu.VMEM((10, p, p), f32)],
        compiler_params=pltpu.CompilerParams(vmem_limit_bytes=16 << 20),
        name="tree",
    )(*arrays)


def gathered(omega, dev_count):
    n_local = omega.shape[0]
    half = n_local // 2
    masks = [2**bit for bit in range(1, dev_count.bit_length() - 1)]
    waves = {}
    for order, first in ((masks, 0), (masks[::-1], half)):
        held = [(0, 0, omega[first : first + half])]
        for place, mask in enumerate(order):
            new = [
                (max(level, place) + (seen > 0), seen ^ mask, value) for level, seen, value in held
            ]
            for at, (level, seen, value) in enumerate(new):
                new[at] = (level, seen, swapped(value, "dev", mask))
            for level, seen, value in new:
                waves.setdefault(level, []).append((seen, first, value))
            held = held + new
    other = swapped(omega, "dev", 1)
    order = [mask * n_local + q for mask in (0, 1) for q in range(n_local)]
    groups = [[omega, other]]
    for level in sorted(waves):
        wave = waves[level]
        for flip in (0, 1):
            for seen, first, value in wave:
                order.extend((seen ^ flip) * n_local + first + q for q in range(half))

        values = [value for _, _, value in wave]
        groups.append(values + [swapped(value, "dev", 1) for value in values])
    return groups, order


def on_device(omega, u_factor, v_factor, columns, ranks):
    n_local, n_blocks = u_factor.shape[1:3]
    leaf_rows, width = u_factor.shape[3:]
    p = omega.shape[3]
    dev_count = lax.axis_size("dev")
    grp_count = lax.axis_size("grp")
    assert n_local == grp_count == 4
    clusters = n_local * dev_count
    most = -(-11 * n_local * n_blocks // (10 * clusters))
    v = jnp.swapaxes(v_factor[0], 2, 3).reshape(n_local * n_blocks, width, leaf_rows)
    u = jnp.swapaxes(u_factor[0], 2, 3).reshape(n_local * n_blocks, width, leaf_rows)
    groups, order = gathered(omega[0], dev_count)
    depth = -(-most // 8) * 8
    unit = 2 * width
    columns = jnp.swapaxes(columns[0], 1, 2)
    slots = slot_table(tuple(order), columns, ranks[0], depth, unit, n_local)
    coeff = None
    start = 0
    for pieces in groups:
        coeff = coefficients(slots, v, pieces, start, most, unit, coeff)
        start += sum(piece.shape[0] for piece in pieces)
    across = swapped(sketch(coeff, u, 3, n_blocks), "grp", 1)
    beside = swapped(sketch(coeff, u, 1, n_blocks), "grp", 1)
    across = swapped(sketch(coeff, u, 2, n_blocks) + across, "grp", 2)
    near, far, rows_own = gram_of([sketch(coeff, u, 0, n_blocks), beside, across], grp_count)
    quarter = rows_own.shape[0]
    far_in = swapped(far, "grp", 2)
    near_in = swapped(near, "grp", 1)
    pass_in = swapped(near_in[quarter:], "grp", 2)
    grams = [far[:p], near_in[quarter : quarter + p], far_in[:p], pass_in[:p]]
    rows_in = [rows_own, near_in[:quarter], far_in[p:], pass_in[p:]]
    current = (grams[0] + grams[1]) + (grams[2] + grams[3])
    lefts, rights = [], []
    for level in range(dev_count.bit_length() - 1):
        lefts.append(current)
        rights.append(swapped(current, "dev", 2**level))
        current = lefts[-1] + rights[-1]
    return tree(grams, rows_in, lefts, rights)


def solution(mesh):
    placed = (
        P("grp", "dev", None, None),
        P("grp", "dev", None, None, None),
        P("grp", "dev", None, None, None),
        P("grp", "dev", None, None),
        P("grp", "dev", None),
    )
    return jax.shard_map(
        on_device,
        mesh=mesh,
        in_specs=placed,
        out_specs=(P("dev", "grp", None), P("dev", None, None)),
        check_vma=False,
    )
```

```python
import functools

import jax
import jax.numpy as jnp
from jax import lax
from jax.experimental import pallas as pl
from jax.experimental.pallas import tpu as pltpu
from jax.sharding import PartitionSpec as P


f32 = jnp.float32
bf16 = jnp.bfloat16
VM = pl.BlockSpec(memory_space=pltpu.VMEM)
SM = pl.BlockSpec(memory_space=pltpu.SMEM)


def swapped(value, axis, mask):
    pairs = [(source, source ^ mask) for source in range(lax.axis_size(axis))]
    return lax.ppermute(value, axis, pairs)


def split(x):
    high = x.astype(bf16)
    low = (x - high.astype(f32)).astype(bf16)
    return high, low


def dot_full(x, y, dims):
    return lax.dot_general(
        x, y, (dims, ((), ())), precision=lax.Precision.HIGHEST, preferred_element_type=f32
    )


def table_kernel(order, unit, n_local, cols_ref, ranks_ref, v_ref, slot_ref, held_ref, sem):
    copy = pltpu.make_async_copy(v_ref, held_ref, sem)
    copy.start()
    n_leaf, _, n_blocks = cols_ref.shape
    depth, clusters = slot_ref.shape
    position = lax.broadcasted_iota(jnp.int32, (clusters, 1), 0)
    names = jnp.zeros((clusters, 1), jnp.int32)
    for at, cluster in enumerate(order):
        names = jnp.where(position == at, cluster, names)
    names = jnp.bitwise_xor(names, lax.axis_index("dev") * n_local)
    ones = jnp.ones((n_blocks, n_blocks), bf16)
    si = lax.broadcasted_iota(jnp.int32, (n_blocks, n_blocks), 0)
    li = lax.broadcasted_iota(jnp.int32, (n_blocks, n_blocks), 1)
    before = jnp.where(si < li, 1.0, 0.0).astype(bf16)
    number = lax.broadcasted_iota(jnp.int32, (depth, n_blocks), 1).astype(f32)
    level = lax.broadcasted_iota(jnp.int32, (depth, n_blocks), 0).astype(f32)
    offset = jnp.zeros((clusters, n_blocks), f32)
    index = jnp.zeros((depth, clusters), f32)
    rank = jnp.zeros((depth, clusters), f32)
    used = jnp.zeros((depth, clusters), f32)
    for c in range(n_leaf):
        named = jnp.where(cols_ref[c] == names, 1.0, 0.0)
        named_low = named.astype(bf16)

        def listed(x, named_low=named_low):
            return lax.dot_general(
                x.astype(bf16), named_low, (((1,), (1,)), ((), ())), preferred_element_type=f32
            )

        ahead = offset + jnp.dot(named_low, before, preferred_element_type=f32)
        place = jnp.sum(named * ahead, axis=0, keepdims=True)
        mark = jnp.where(place == level, 1.0, 0.0)
        here = listed(mark)
        index = index + listed(mark * number) + here * float(c * n_blocks)
        rank = rank + listed(mark * ranks_ref[c : c + 1, :].astype(f32))
        used = used + here
        offset = offset + jnp.dot(named_low, ones, preferred_element_type=f32)
    index = jnp.where(used > 0.5, index, float(n_leaf * n_blocks))
    slot_ref[...] = index.astype(jnp.int32) * unit + rank.astype(jnp.int32)
    copy.wait()


def slot_table(order, cols, ranks, v, depth, unit, n_local):
    return pl.pallas_call(
        functools.partial(table_kernel, order, unit, n_local),
        out_shape=(
            jax.ShapeDtypeStruct((depth, len(order)), jnp.int32),
            jax.ShapeDtypeStruct(v.shape, f32),
        ),
        in_specs=[VM, VM, pl.BlockSpec(memory_space=pltpu.HBM)],
        out_specs=(VM, VM),
        scratch_shapes=[pltpu.SemaphoreType.DMA],
        compiler_params=pltpu.CompilerParams(vmem_limit_bytes=4 << 20),
        cost_estimate=pl.CostEstimate(flops=0, bytes_accessed=24 << 20, transcendentals=0),
        name="slots",
    )(cols, ranks, v)


def coeff_kernel(most, start, unit, n_pieces, *refs):
    slot_ref, v_ref = refs[:2]
    pieces = refs[2 : 2 + n_pieces]
    c_ref, w_ref = refs[-2:]
    p = pieces[0].shape[2]
    n_all, k, _ = v_ref.shape
    at = 0
    for piece in pieces:
        for q in range(piece.shape[0]):
            high, low = split(piece[q])
            w_ref[at, :, :p] = high
            w_ref[at, :, p:] = low
            at += 1
    sub = lax.broadcasted_iota(jnp.int32, (k, p), 0)

    def body(j, _):
        highs, lows, ids, kept = [], [], [], []
        for n in range(most):
            entry = slot_ref[n, start + j]
            b = entry // unit
            ids.append(b)
            kept.append(sub < entry % unit)
            high, low = split(v_ref[jnp.minimum(b, n_all - 1)])
            highs.append(high)
            lows.append(low)
        w = w_ref[j]
        both = jnp.dot(jnp.concatenate(highs, 0), w, preferred_element_type=f32)
        both = both + jnp.dot(jnp.concatenate(lows, 0), w, preferred_element_type=f32)
        total = both[:, :p] + both[:, p:]
        for n in range(most):
            c_ref[ids[n]] = jnp.where(kept[n], total[n * k : (n + 1) * k], 0.0)
        return 0

    lax.fori_loop(0, at, body, 0, unroll=4)


def coefficients(slots, v, pieces, start, most, unit, before):
    n_all, k, rows = v.shape
    p = pieces[0].shape[2]
    held = sum(piece.shape[0] for piece in pieces)
    chained = before is not None
    args = [slots, v, *pieces] + ([before] if chained else [])
    return pl.pallas_call(
        functools.partial(coeff_kernel, most, start, unit, len(pieces)),
        out_shape=jax.ShapeDtypeStruct((n_all + 1, k, p), f32),
        in_specs=[SM, VM] + [VM] * len(pieces) + [VM] * chained,
        out_specs=VM,
        scratch_shapes=[pltpu.VMEM((held, rows, 2 * p), bf16)],
        input_output_aliases={len(args) - 1: 0} if chained else {},
        compiler_params=pltpu.CompilerParams(vmem_limit_bytes=12 << 20),
        cost_estimate=pl.CostEstimate(
            flops=held * most * k * rows * p * 8, bytes_accessed=8 << 20, transcendentals=0
        ),
        name="coeff",
    )(*args)


def sketch_kernel(m, n_blocks, c_ref, u_ref, o_ref):
    p, rows = o_ref.shape
    k = u_ref.shape[1]
    step = rows // k
    leaf = jnp.bitwise_xor(lax.axis_index("grp"), m)
    total = jnp.zeros((p, rows), f32)
    for q in range(n_blocks // step):
        at = pl.ds(leaf * n_blocks + q * step, step)
        high, low = split(c_ref[at].reshape(rows, p).T)
        u_high, u_low = split(u_ref[at].reshape(rows, rows))
        total = total + jnp.dot(high, u_high, preferred_element_type=f32)
        total = total + jnp.dot(low, u_high, preferred_element_type=f32)
        total = total + jnp.dot(high, u_low, preferred_element_type=f32)
    o_ref[...] = total


def sketch(coeff, u, m, n_blocks):
    k, rows = u.shape[1:]
    p = coeff.shape[2]
    return pl.pallas_call(
        functools.partial(sketch_kernel, m, n_blocks),
        out_shape=jax.ShapeDtypeStruct((p, rows), f32),
        in_specs=[VM, VM],
        out_specs=VM,
        compiler_params=pltpu.CompilerParams(vmem_limit_bytes=8 << 20),
        cost_estimate=pl.CostEstimate(
            flops=n_blocks * k * rows * p * 6, bytes_accessed=1 << 20, transcendentals=0
        ),
        name="sketch",
    )(coeff, u)


def pack(gram):
    p = gram.shape[0]
    half = p // 2
    ri = lax.broadcasted_iota(jnp.int32, (half, p), 0)
    ci = lax.broadcasted_iota(jnp.int32, (half, p), 1)
    lower = gram[half:]
    body = jnp.where(ci < ri, pltpu.roll(lower, half, 1), gram[:half])
    diagonal = jnp.sum(jnp.where(ci == ri + half, lower, 0.0), axis=0, keepdims=True)
    return body, jnp.broadcast_to(diagonal, (8, p))


def unpack(packed):
    p = packed.shape[1]
    half = p // 2
    ri = lax.broadcasted_iota(jnp.int32, (half, p), 0)
    ci = lax.broadcasted_iota(jnp.int32, (half, p), 1)
    body = packed[:half]
    upper = jnp.where(ci >= ri, body, 0.0)
    lower = jnp.where((ci >= half) & (ci - half < ri), pltpu.roll(body, half, 1), 0.0)
    lower = jnp.where(ci == ri + half, packed[half : half + 1], lower)
    once = jnp.concatenate([upper, lower], axis=0)
    rj = lax.broadcasted_iota(jnp.int32, (p, p), 0)
    cj = lax.broadcasted_iota(jnp.int32, (p, p), 1)
    return jnp.where(rj == cj, once, once + once.T)


def gram_kernel(n_terms, *refs):
    terms = refs[:n_terms]
    near_ref, far_ref, rows_ref, keep_ref, hold_ref = refs[n_terms:]
    total = terms[0][...]
    for term in terms[1:]:
        total = total + term[...]
    body, diagonal = pack(dot_full(total, total, ((1,), (1,))))
    half = body.shape[0]
    far_ref[:half] = body
    far_ref[half:] = diagonal
    hold_ref[...] = total.T
    quarter = keep_ref.shape[0]

    def rows_of(m):
        at = pl.multiple_of(jnp.bitwise_xor(lax.axis_index("grp"), m) * quarter, quarter)
        return hold_ref[pl.ds(at, quarter), :]

    near_ref[:quarter] = rows_of(1)
    near_ref[quarter : quarter + half] = body
    near_ref[quarter + half : quarter + half + 8] = diagonal
    near_ref[quarter + half + 8 :] = rows_of(3)
    rows_ref[...] = rows_of(2)
    keep_ref[...] = rows_of(0)


def gram_of(terms, n_grp):
    p, rows = terms[0].shape
    quarter = rows // n_grp
    short = p // 2 + 8
    return pl.pallas_call(
        functools.partial(gram_kernel, len(terms)),
        out_shape=tuple(
            jax.ShapeDtypeStruct((height, p), f32)
            for height in (short + 2 * quarter, short, quarter, quarter)
        ),
        in_specs=[VM] * len(terms),
        out_specs=(VM, VM, VM, VM),
        scratch_shapes=[pltpu.VMEM((rows, p), f32)],
        compiler_params=pltpu.CompilerParams(vmem_limit_bytes=8 << 20),
        name="gram",
    )(*terms)


def factor(m_ref, panel, group):
    count, p, _ = m_ref.shape
    lane = lax.broadcasted_iota(jnp.int32, (1, 1, p), 2)
    sub8 = lax.broadcasted_iota(jnp.int32, (1, 8, p), 1)
    n_tiles = panel // 8
    for base in range(0, p, panel):
        after = base + panel
        x = [m_ref[:, base + 8 * i : base + 8 * i + 8, :] for i in range(n_tiles)]
        for t0 in range(0, panel, group):
            i0 = t0 // 8
            tiles = range(i0, n_tiles)
            columns = []
            for s in range(t0, t0 + group):
                k = base + s
                columns.append([jnp.broadcast_to(x[i][:, :, k : k + 1], x[i].shape) for i in tiles])
            for t in range(group):
                ts = (t0 + t) % 8
                hit = lane == base + t0 + t
                scale = lax.rsqrt(columns[t][0][:, ts : ts + 1, :])
                parts = [column * scale for column in columns[t]]
                for s in range(t + 1, group):
                    ss = (t0 + s) % 8
                    weight = parts[0][:, ss : ss + 1, :]
                    columns[s] = [c - part * weight for c, part in zip(columns[s], parts)]
                row = jnp.where(hit, 1.0, x[i0][:, ts : ts + 1, :]) * scale
                for i in tiles:
                    new = jnp.where(hit, 0.0, x[i]) - parts[i - i0] * row
                    if i == i0:
                        new = jnp.where(sub8 < ts, x[i], jnp.where(sub8 == ts, row, new))
                    x[i] = new
        for i in range(n_tiles):
            m_ref[:, base + 8 * i : base + 8 * i + 8, :] = x[i]
        if after < p:
            for b in range(count):
                block = m_ref[b, base:after, :]
                si = lax.broadcasted_iota(jnp.int32, block.shape, 0)
                li = lax.broadcasted_iota(jnp.int32, block.shape, 1)
                right = jnp.where((li < after) & (li - base > si), 0.0, block)
                change = dot_full(block.T[after:, :], right, ((1,), (0,)))
                old = m_ref[b, after:, :]
                lj = lax.broadcasted_iota(jnp.int32, old.shape, 1)
                old = jnp.where((lj >= base) & (lj < after), 0.0, old)
                m_ref[b, after:, :] = old - change


def tree_kernel(panel, group, n_leaf, n_levels, *refs):
    grams = refs[:n_leaf]
    rows_in = refs[n_leaf : 2 * n_leaf]
    lefts = refs[2 * n_leaf : 2 * n_leaf + n_levels]
    rights = refs[2 * n_leaf + n_levels : 2 * n_leaf + 2 * n_levels]
    basis_ref, tr_ref, m_ref, pick_ref = refs[2 * n_leaf + 2 * n_levels :]
    p = m_ref.shape[1]
    own = lax.axis_index("grp")
    device = lax.axis_index("dev")
    for m in range(n_leaf):
        m_ref[jnp.bitwise_xor(own, m)] = unpack(grams[m][...])
    m_ref[4] = m_ref[0] + m_ref[1]
    m_ref[5] = m_ref[2] + m_ref[3]
    m_ref[6] = m_ref[4] + m_ref[5]
    pick_ref[0] = grams[0][...]
    pick_ref[1] = grams[1][...]
    for level in range(n_levels):

        @pl.when(device % 2 ** (level + 1) == 2**level - 1)
        def _(level=level):
            pick_ref[0] = lefts[level][...]
            pick_ref[1] = rights[level][...]

    m_ref[7] = unpack(pick_ref[0])
    m_ref[8] = unpack(pick_ref[1])
    m_ref[9] = m_ref[7] + m_ref[8]
    factor(m_ref, panel, group)
    ri = lax.broadcasted_iota(jnp.int32, (p, p), 0)
    ci = lax.broadcasted_iota(jnp.int32, (p, p), 1)

    def inverse(b):
        return jnp.concatenate(split(jnp.where(ci <= ri, m_ref[b], 0.0)), axis=0)

    def upper(b):
        whole = m_ref[b]
        return jnp.where(ci > ri, whole, jnp.where(ci == ri, 1.0 / whole, 0.0))

    def applied(x, solve):
        high, low = split(x)
        dims = (((1,), (1,)), ((), ()))
        both = lax.dot_general(high, solve, dims, preferred_element_type=f32)
        both = both + lax.dot_general(low, solve, dims, preferred_element_type=f32)
        return both[:, :p] + both[:, p:]

    for m in range(n_leaf):
        leaf = jnp.bitwise_xor(own, m)
        basis_ref[leaf] = applied(rows_in[m][...], inverse(leaf))
    keep = device != lax.axis_size("dev") - 1
    for q, (a, b, node) in enumerate(((0, 1, 4), (2, 3, 5), (4, 5, 6), (7, 8, 9))):
        made = applied(jnp.concatenate([upper(a), upper(b)], axis=0), inverse(node))
        tr_ref[q] = jnp.where(keep, made, 0.0) if q == 3 else made


def tree(grams, rows_in, lefts, rights, panel=32, group=4):
    quarter, p = rows_in[0].shape
    n_leaf = len(grams)
    arrays = [*grams, *rows_in, *lefts, *rights]
    return pl.pallas_call(
        functools.partial(tree_kernel, panel, group, n_leaf, len(lefts)),
        out_shape=(
            jax.ShapeDtypeStruct((n_leaf, quarter, p), f32),
            jax.ShapeDtypeStruct((4, 2 * p, p), f32),
        ),
        in_specs=[VM] * len(arrays),
        out_specs=(VM, VM),
        scratch_shapes=[pltpu.VMEM((10, p, p), f32), pltpu.VMEM((2, *grams[0].shape), f32)],
        compiler_params=pltpu.CompilerParams(vmem_limit_bytes=16 << 20),
        name="tree",
    )(*arrays)


def gathered(omega, dev_count):
    n_local = omega.shape[0]
    half = n_local // 2
    masks = [2**bit for bit in range(1, dev_count.bit_length() - 1)]
    waves = {}
    for order, first in ((masks, 0), (masks[::-1], half)):
        held = [(0, 0, omega[first : first + half])]
        for place, mask in enumerate(order):
            new = [
                (max(level, place) + (seen > 0), seen ^ mask, value) for level, seen, value in held
            ]
            for at, (level, seen, value) in enumerate(new):
                new[at] = (level, seen, swapped(value, "dev", mask))
            for level, seen, value in new:
                waves.setdefault(level, []).append((seen, first, value))
            held = held + new
    other = swapped(omega, "dev", 1)
    order = [mask * n_local + q for mask in (0, 1) for q in range(n_local)]
    groups = [[omega[:half], omega[half:], other]]
    for level in sorted(waves):
        wave = waves[level]
        for flip in (0, 1):
            for seen, first, value in wave:
                order.extend((seen ^ flip) * n_local + first + q for q in range(half))

        values = [value for _, _, value in wave]
        groups.append(values + [swapped(value, "dev", 1) for value in values])
    return groups, order


def on_device(omega, u_factor, v_factor, columns, ranks):
    n_local, n_blocks = u_factor.shape[1:3]
    leaf_rows, width = u_factor.shape[3:]
    dev_count = lax.axis_size("dev")
    grp_count = lax.axis_size("grp")
    assert n_local == grp_count == 4
    clusters = n_local * dev_count
    most = -(-11 * n_local * n_blocks // (10 * clusters))
    v = jnp.swapaxes(v_factor[0], 2, 3).reshape(n_local * n_blocks, width, leaf_rows)
    u = jnp.swapaxes(u_factor[0], 2, 3).reshape(n_local * n_blocks, width, leaf_rows)
    groups, order = gathered(omega[0], dev_count)
    depth = -(-most // 8) * 8
    unit = 2 * width
    columns = jnp.swapaxes(columns[0], 1, 2)
    slots, v = slot_table(tuple(order), columns, ranks[0], v, depth, unit, n_local)
    coeff = None
    start = 0
    for pieces in groups:
        coeff = coefficients(slots, v, pieces, start, most, unit, coeff)
        start += sum(piece.shape[0] for piece in pieces)
    across = swapped(sketch(coeff, u, 3, n_blocks), "grp", 1)
    beside = swapped(sketch(coeff, u, 1, n_blocks), "grp", 1)
    across = swapped(sketch(coeff, u, 2, n_blocks) + across, "grp", 2)
    near, far, rows_far, rows_own = gram_of(
        [sketch(coeff, u, 0, n_blocks), beside, across], grp_count
    )
    quarter, short = rows_own.shape[0], far.shape[0]
    near_in = swapped(near, "grp", 1)
    far_in = swapped(far, "grp", 2)
    gram_in = near_in[quarter : quarter + short]
    pass_in = swapped(gram_in, "grp", 2)
    grams = [far, gram_in, far_in, pass_in]
    current = (far + gram_in) + (far_in + pass_in)
    lefts, rights = [], []
    masks = [2**bit for bit in range(dev_count.bit_length() - 1)]
    steps = [masks[:1]] + [masks[at : at + 2] for at in range(1, len(masks), 2)]
    for step in steps:
        first = swapped(current, "dev", step[0])
        wider = [swapped(current, "dev", extra ^ step[1]) for extra in (0, step[0])] if step[1:] else []
        lefts.append(current)
        rights.append(first)
        current = current + first
        if wider:
            lefts.append(current)
            rights.append(wider[0] + wider[1])
            current = current + rights[-1]
    both_in = swapped(jnp.concatenate([rows_far, near_in[quarter + short :]]), "grp", 2)
    rows_in = [rows_own, near_in[:quarter], both_in[:quarter], both_in[quarter:]]
    return tree(grams, rows_in, lefts, rights)


def solution(mesh):
    placed = (
        P("grp", "dev", None, None),
        P("grp", "dev", None, None, None),
        P("grp", "dev", None, None, None),
        P("grp", "dev", None, None),
        P("grp", "dev", None),
    )
    return jax.shard_map(
        on_device,
        mesh=mesh,
        in_specs=placed,
        out_specs=(P("dev", "grp", None), P("dev", None, None)),
        check_vma=False,
    )
```

```python
import functools

import jax
import jax.numpy as jnp
from jax import lax
from jax.experimental import pallas as pl
from jax.experimental.pallas import tpu as pltpu
from jax.sharding import PartitionSpec as P


f32 = jnp.float32
bf16 = jnp.bfloat16
VM = pl.BlockSpec(memory_space=pltpu.VMEM)
SM = pl.BlockSpec(memory_space=pltpu.SMEM)


def swapped(value, axis, mask):
    pairs = [(source, source ^ mask) for source in range(lax.axis_size(axis))]
    return lax.ppermute(value, axis, pairs)


def split(x):
    high = x.astype(bf16)
    low = (x - high.astype(f32)).astype(bf16)
    return high, low


def dot_full(x, y, dims):
    return lax.dot_general(
        x, y, (dims, ((), ())), precision=lax.Precision.HIGHEST, preferred_element_type=f32
    )


def table_kernel(order, unit, n_local, cols_ref, ranks_ref, v_ref, slot_ref, held_ref, sem):
    copy = pltpu.make_async_copy(v_ref, held_ref, sem)
    copy.start()
    n_leaf, _, n_blocks = cols_ref.shape
    depth, clusters = slot_ref.shape
    position = lax.broadcasted_iota(jnp.int32, (clusters, 1), 0)
    names = jnp.zeros((clusters, 1), jnp.int32)
    for at, cluster in enumerate(order):
        names = jnp.where(position == at, cluster, names)
    names = jnp.bitwise_xor(names, lax.axis_index("dev") * n_local)
    ones = jnp.ones((n_blocks, n_blocks), bf16)
    si = lax.broadcasted_iota(jnp.int32, (n_blocks, n_blocks), 0)
    li = lax.broadcasted_iota(jnp.int32, (n_blocks, n_blocks), 1)
    before = jnp.where(si < li, 1.0, 0.0).astype(bf16)
    number = lax.broadcasted_iota(jnp.int32, (depth, n_blocks), 1).astype(f32)
    level = lax.broadcasted_iota(jnp.int32, (depth, n_blocks), 0).astype(f32)
    offset = jnp.zeros((clusters, n_blocks), f32)
    index = jnp.zeros((depth, clusters), f32)
    rank = jnp.zeros((depth, clusters), f32)
    used = jnp.zeros((depth, clusters), f32)
    for c in range(n_leaf):
        named = jnp.where(cols_ref[c] == names, 1.0, 0.0)
        named_low = named.astype(bf16)

        def listed(x, named_low=named_low):
            return lax.dot_general(
                x.astype(bf16), named_low, (((1,), (1,)), ((), ())), preferred_element_type=f32
            )

        ahead = offset + jnp.dot(named_low, before, preferred_element_type=f32)
        place = jnp.sum(named * ahead, axis=0, keepdims=True)
        mark = jnp.where(place == level, 1.0, 0.0)
        here = listed(mark)
        index = index + listed(mark * number) + here * float(c * n_blocks)
        rank = rank + listed(mark * ranks_ref[c : c + 1, :].astype(f32))
        used = used + here
        offset = offset + jnp.dot(named_low, ones, preferred_element_type=f32)
    index = jnp.where(used > 0.5, index, float(n_leaf * n_blocks))
    slot_ref[...] = index.astype(jnp.int32) * unit + rank.astype(jnp.int32)
    copy.wait()


def slot_table(order, cols, ranks, v, depth, unit, n_local):
    return pl.pallas_call(
        functools.partial(table_kernel, order, unit, n_local),
        out_shape=(
            jax.ShapeDtypeStruct((depth, len(order)), jnp.int32),
            jax.ShapeDtypeStruct(v.shape, f32),
        ),
        in_specs=[VM, VM, pl.BlockSpec(memory_space=pltpu.HBM)],
        out_specs=(VM, VM),
        scratch_shapes=[pltpu.SemaphoreType.DMA],
        compiler_params=pltpu.CompilerParams(vmem_limit_bytes=38 << 20),
        cost_estimate=pl.CostEstimate(flops=0, bytes_accessed=24 << 20, transcendentals=0),
        name="slots",
    )(cols, ranks, v)


def coeff_kernel(most, start, unit, n_pieces, *refs):
    slot_ref, v_ref = refs[:2]
    pieces = refs[2 : 2 + n_pieces]
    c_ref, w_ref = refs[-2:]
    p = pieces[0].shape[2]
    n_all, k, _ = v_ref.shape
    at = 0
    for piece in pieces:
        for q in range(piece.shape[0]):
            high, low = split(piece[q])
            w_ref[at, :, :p] = high
            w_ref[at, :, p:] = low
            at += 1
    sub = lax.broadcasted_iota(jnp.int32, (k, p), 0)

    def body(j, _):
        highs, lows, ids, kept = [], [], [], []
        for n in range(most):
            entry = slot_ref[n, start + j]
            b = entry // unit
            ids.append(b)
            kept.append(sub < entry % unit)
            high, low = split(v_ref[jnp.minimum(b, n_all - 1)])
            highs.append(high)
            lows.append(low)
        w = w_ref[j]
        both = jnp.dot(jnp.concatenate(highs, 0), w, preferred_element_type=f32)
        both = both + jnp.dot(jnp.concatenate(lows, 0), w, preferred_element_type=f32)
        total = both[:, :p] + both[:, p:]
        for n in range(most):
            c_ref[ids[n]] = jnp.where(kept[n], total[n * k : (n + 1) * k], 0.0)
        return 0

    lax.fori_loop(0, at, body, 0, unroll=4)


def coefficients(slots, v, pieces, start, most, unit, before):
    n_all, k, rows = v.shape
    p = pieces[0].shape[2]
    held = sum(piece.shape[0] for piece in pieces)
    chained = before is not None
    args = [slots, v, *pieces] + ([before] if chained else [])
    return pl.pallas_call(
        functools.partial(coeff_kernel, most, start, unit, len(pieces)),
        out_shape=jax.ShapeDtypeStruct((n_all + 1, k, p), f32),
        in_specs=[SM, VM] + [VM] * len(pieces) + [VM] * chained,
        out_specs=VM,
        scratch_shapes=[pltpu.VMEM((held, rows, 2 * p), bf16)],
        input_output_aliases={len(args) - 1: 0} if chained else {},
        compiler_params=pltpu.CompilerParams(vmem_limit_bytes=12 << 20),
        cost_estimate=pl.CostEstimate(
            flops=held * most * k * rows * p * 8, bytes_accessed=8 << 20, transcendentals=0
        ),
        name="coeff",
    )(*args)


def sketch_kernel(m, n_blocks, c_ref, u_ref, o_ref):
    p, rows = o_ref.shape
    k = u_ref.shape[1]
    step = rows // k
    leaf = jnp.bitwise_xor(lax.axis_index("grp"), m)
    total = jnp.zeros((p, rows), f32)
    for q in range(n_blocks // step):
        at = pl.ds(leaf * n_blocks + q * step, step)
        high, low = split(c_ref[at].reshape(rows, p).T)
        u_high, u_low = split(u_ref[at].reshape(rows, rows))
        total = total + jnp.dot(high, u_high, preferred_element_type=f32)
        total = total + jnp.dot(low, u_high, preferred_element_type=f32)
        total = total + jnp.dot(high, u_low, preferred_element_type=f32)
    o_ref[...] = total


def sketch(coeff, u, m, n_blocks):
    k, rows = u.shape[1:]
    p = coeff.shape[2]
    return pl.pallas_call(
        functools.partial(sketch_kernel, m, n_blocks),
        out_shape=jax.ShapeDtypeStruct((p, rows), f32),
        in_specs=[VM, VM],
        out_specs=VM,
        compiler_params=pltpu.CompilerParams(vmem_limit_bytes=8 << 20),
        cost_estimate=pl.CostEstimate(
            flops=n_blocks * k * rows * p * 6, bytes_accessed=1 << 20, transcendentals=0
        ),
        name="sketch",
    )(coeff, u)


def pack(gram):
    p = gram.shape[0]
    half = p // 2
    ri = lax.broadcasted_iota(jnp.int32, (half, p), 0)
    ci = lax.broadcasted_iota(jnp.int32, (half, p), 1)
    lower = gram[half:]
    body = jnp.where(ci < ri, pltpu.roll(lower, half, 1), gram[:half])
    diagonal = jnp.sum(jnp.where(ci == ri + half, lower, 0.0), axis=0, keepdims=True)
    return body, jnp.broadcast_to(diagonal, (8, p))


def unpack(packed):
    p = packed.shape[1]
    half = p // 2
    ri = lax.broadcasted_iota(jnp.int32, (half, p), 0)
    ci = lax.broadcasted_iota(jnp.int32, (half, p), 1)
    body = packed[:half]
    upper = jnp.where(ci >= ri, body, 0.0)
    lower = jnp.where((ci >= half) & (ci - half < ri), pltpu.roll(body, half, 1), 0.0)
    lower = jnp.where(ci == ri + half, packed[half : half + 1], lower)
    once = jnp.concatenate([upper, lower], axis=0)
    rj = lax.broadcasted_iota(jnp.int32, (p, p), 0)
    cj = lax.broadcasted_iota(jnp.int32, (p, p), 1)
    return jnp.where(rj == cj, once, once + once.T)


def gram_kernel(n_terms, *refs):
    terms = refs[:n_terms]
    gram_ref, near_ref, far_ref, keep_ref, hold_ref = refs[n_terms:]
    total = terms[0][...]
    for term in terms[1:]:
        total = total + term[...]
    body, diagonal = pack(dot_full(total, total, ((1,), (1,))))
    half = body.shape[0]
    gram_ref[:half] = body
    gram_ref[half:] = diagonal
    hold_ref[...] = total.T
    quarter = keep_ref.shape[0]

    def rows_of(m):
        at = pl.multiple_of(jnp.bitwise_xor(lax.axis_index("grp"), m) * quarter, quarter)
        return hold_ref[pl.ds(at, quarter), :]

    near_ref[:quarter] = rows_of(1)
    near_ref[quarter:] = rows_of(3)
    far_ref[...] = rows_of(2)
    keep_ref[...] = rows_of(0)


def gram_of(terms, n_grp):
    p, rows = terms[0].shape
    quarter = rows // n_grp
    return pl.pallas_call(
        functools.partial(gram_kernel, len(terms)),
        out_shape=tuple(
            jax.ShapeDtypeStruct((height, p), f32)
            for height in (p // 2 + 8, 2 * quarter, quarter, quarter)
        ),
        in_specs=[VM] * len(terms),
        out_specs=(VM, VM, VM, VM),
        scratch_shapes=[pltpu.VMEM((rows, p), f32)],
        compiler_params=pltpu.CompilerParams(vmem_limit_bytes=8 << 20),
        name="gram",
    )(*terms)


def factor(m_ref, panel, group):
    count, p, _ = m_ref.shape
    lane = lax.broadcasted_iota(jnp.int32, (1, 1, p), 2)
    sub8 = lax.broadcasted_iota(jnp.int32, (1, 8, p), 1)
    n_tiles = panel // 8
    for base in range(0, p, panel):
        after = base + panel
        x = [m_ref[:, base + 8 * i : base + 8 * i + 8, :] for i in range(n_tiles)]
        for t0 in range(0, panel, group):
            i0 = t0 // 8
            tiles = range(i0, n_tiles)
            columns = []
            for s in range(t0, t0 + group):
                k = base + s
                columns.append([jnp.broadcast_to(x[i][:, :, k : k + 1], x[i].shape) for i in tiles])
            for t in range(group):
                ts = (t0 + t) % 8
                hit = lane == base + t0 + t
                scale = lax.rsqrt(columns[t][0][:, ts : ts + 1, :])
                parts = [column * scale for column in columns[t]]
                for s in range(t + 1, group):
                    ss = (t0 + s) % 8
                    weight = parts[0][:, ss : ss + 1, :]
                    columns[s] = [c - part * weight for c, part in zip(columns[s], parts)]
                row = jnp.where(hit, 1.0, x[i0][:, ts : ts + 1, :]) * scale
                for i in tiles:
                    new = jnp.where(hit, 0.0, x[i]) - parts[i - i0] * row
                    if i == i0:
                        new = jnp.where(sub8 < ts, x[i], jnp.where(sub8 == ts, row, new))
                    x[i] = new
        for i in range(n_tiles):
            m_ref[:, base + 8 * i : base + 8 * i + 8, :] = x[i]
        if after < p:
            for b in range(count):
                block = m_ref[b, base:after, :]
                si = lax.broadcasted_iota(jnp.int32, block.shape, 0)
                li = lax.broadcasted_iota(jnp.int32, block.shape, 1)
                right = jnp.where((li < after) & (li - base > si), 0.0, block)
                change = dot_full(block.T[after:, :], right, ((1,), (0,)))
                old = m_ref[b, after:, :]
                lj = lax.broadcasted_iota(jnp.int32, old.shape, 1)
                old = jnp.where((lj >= base) & (lj < after), 0.0, old)
                m_ref[b, after:, :] = old - change


def applied(x, solve):
    p = x.shape[1]
    high, low = split(x)
    dims = (((1,), (1,)), ((), ()))
    both = lax.dot_general(high, solve, dims, preferred_element_type=f32)
    both = both + lax.dot_general(low, solve, dims, preferred_element_type=f32)
    return both[:, :p] + both[:, p:]


def tree_kernel(panel, group, n_leaf, n_levels, *refs):
    grams = refs[:n_leaf]
    lefts = refs[n_leaf : n_leaf + n_levels]
    rights = refs[n_leaf + n_levels : n_leaf + 2 * n_levels]
    solve_ref, tr_ref, m_ref, pick_ref = refs[n_leaf + 2 * n_levels :]
    p = m_ref.shape[1]
    own = lax.axis_index("grp")
    device = lax.axis_index("dev")
    for m in range(n_leaf):
        m_ref[jnp.bitwise_xor(own, m)] = unpack(grams[m][...])
    m_ref[4] = m_ref[0] + m_ref[1]
    m_ref[5] = m_ref[2] + m_ref[3]
    m_ref[6] = m_ref[4] + m_ref[5]
    pick_ref[0] = grams[0][...]
    pick_ref[1] = grams[1][...]
    for level in range(n_levels):

        @pl.when(device % 2 ** (level + 1) == 2**level - 1)
        def _(level=level):
            pick_ref[0] = lefts[level][...]
            pick_ref[1] = rights[level][...]

    m_ref[7] = unpack(pick_ref[0])
    m_ref[8] = unpack(pick_ref[1])
    m_ref[9] = m_ref[7] + m_ref[8]
    factor(m_ref, panel, group)
    ri = lax.broadcasted_iota(jnp.int32, (p, p), 0)
    ci = lax.broadcasted_iota(jnp.int32, (p, p), 1)

    def inverse(b):
        return jnp.concatenate(split(jnp.where(ci <= ri, m_ref[b], 0.0)), axis=0)

    def upper(b):
        whole = m_ref[b]
        return jnp.where(ci > ri, whole, jnp.where(ci == ri, 1.0 / whole, 0.0))

    for leaf in range(n_leaf):
        solve_ref[leaf] = inverse(leaf)
    keep = device != lax.axis_size("dev") - 1
    for q, (a, b, node) in enumerate(((0, 1, 4), (2, 3, 5), (4, 5, 6), (7, 8, 9))):
        made = applied(jnp.concatenate([upper(a), upper(b)], axis=0), inverse(node))
        tr_ref[q] = jnp.where(keep, made, 0.0) if q == 3 else made


def tree(grams, lefts, rights, panel=32, group=4):
    p = grams[0].shape[1]
    n_leaf = len(grams)
    arrays = [*grams, *lefts, *rights]
    return pl.pallas_call(
        functools.partial(tree_kernel, panel, group, n_leaf, len(lefts)),
        out_shape=(
            jax.ShapeDtypeStruct((n_leaf, 2 * p, p), bf16),
            jax.ShapeDtypeStruct((4, 2 * p, p), f32),
        ),
        in_specs=[VM] * len(arrays),
        out_specs=(VM, VM),
        scratch_shapes=[pltpu.VMEM((10, p, p), f32), pltpu.VMEM((2, *grams[0].shape), f32)],
        compiler_params=pltpu.CompilerParams(vmem_limit_bytes=16 << 20),
        cost_estimate=pl.CostEstimate(flops=0, bytes_accessed=24 << 20, transcendentals=0),
        name="tree",
    )(*arrays)


def basis_kernel(solve_ref, own_ref, near_ref, far_ref, basis_ref):
    own = lax.axis_index("grp")
    quarter = own_ref.shape[0]
    rows = (own_ref[...], near_ref[:quarter], far_ref[:quarter], far_ref[quarter:])
    for m, value in enumerate(rows):
        leaf = jnp.bitwise_xor(own, m)
        basis_ref[leaf] = applied(value, solve_ref[leaf])


def basis(solves, own, near, far):
    n_leaf = solves.shape[0]
    quarter, p = own.shape
    return pl.pallas_call(
        basis_kernel,
        out_shape=jax.ShapeDtypeStruct((n_leaf, quarter, p), f32),
        in_specs=[VM] * 4,
        out_specs=VM,
        compiler_params=pltpu.CompilerParams(vmem_limit_bytes=8 << 20),
        name="basis",
    )(solves, own, near, far)


def gathered(omega, dev_count):
    n_local = omega.shape[0]
    half = n_local // 2
    masks = [2**bit for bit in range(1, dev_count.bit_length() - 1)]
    waves = {}
    for order, first in ((masks, 0), (masks[::-1], half)):
        held = [(0, 0, omega[first : first + half])]
        for place, mask in enumerate(order):
            new = [
                (max(level, place) + (seen > 0), seen ^ mask, value) for level, seen, value in held
            ]
            for at, (level, seen, value) in enumerate(new):
                new[at] = (level, seen, swapped(value, "dev", mask))
            for level, seen, value in new:
                waves.setdefault(level, []).append((seen, first, value))
            held = held + new
    other = swapped(omega, "dev", 1)
    order = [mask * n_local + q for mask in (0, 1) for q in range(n_local)]
    groups = [[omega[:half], omega[half:], other]]
    for level in sorted(waves):
        wave = waves[level]
        for flip in (0, 1):
            for seen, first, value in wave:
                order.extend((seen ^ flip) * n_local + first + q for q in range(half))

        values = [value for _, _, value in wave]
        others = [swapped(value, "dev", 1) for value in values]
        if level < max(waves):
            groups.append(values + others)
        else:
            groups.extend([values, others])
    return groups, order


def on_device(omega, u_factor, v_factor, columns, ranks):
    n_local, n_blocks = u_factor.shape[1:3]
    leaf_rows, width = u_factor.shape[3:]
    dev_count = lax.axis_size("dev")
    grp_count = lax.axis_size("grp")
    assert n_local == grp_count == 4
    clusters = n_local * dev_count
    most = -(-11 * n_local * n_blocks // (10 * clusters))
    v = jnp.swapaxes(v_factor[0], 2, 3).reshape(n_local * n_blocks, width, leaf_rows)
    u = jnp.swapaxes(u_factor[0], 2, 3).reshape(n_local * n_blocks, width, leaf_rows)
    groups, order = gathered(omega[0], dev_count)
    depth = -(-most // 8) * 8
    unit = 2 * width
    columns = jnp.swapaxes(columns[0], 1, 2)
    slots, v = slot_table(tuple(order), columns, ranks[0], v, depth, unit, n_local)
    coeff = None
    start = 0
    for pieces in groups:
        coeff = coefficients(slots, v, pieces, start, most, unit, coeff)
        start += sum(piece.shape[0] for piece in pieces)
    made = {}
    for m in (3, 2, 1, 0):
        made[m] = sketch(coeff, u, m, n_blocks)
    across = swapped(made[3], "grp", 1)
    across = swapped(made[2] + across, "grp", 2)
    beside = swapped(made[1], "grp", 1)
    gram, rows_near, rows_far, rows_own = gram_of([made[0], beside, across], grp_count)
    near_in = swapped(gram, "grp", 1)
    far_in = swapped(gram, "grp", 2)
    pass_in = swapped(near_in, "grp", 2)
    rows_near = swapped(rows_near, "grp", 1)
    grams = [gram, near_in, far_in, pass_in]
    current = (gram + near_in) + (far_in + pass_in)
    lefts, rights = [], []
    masks = [2**bit for bit in range(dev_count.bit_length() - 1)]
    steps = [masks[:1]] + [masks[at : at + 2] for at in range(1, len(masks), 2)]
    for step in steps:
        first = swapped(current, "dev", step[0])
        wider = [swapped(current, "dev", extra ^ step[1]) for extra in (0, step[0])] if step[1:] else []
        lefts.append(current)
        rights.append(first)
        current = current + first
        if wider:
            lefts.append(current)
            rights.append(wider[0] + wider[1])
            current = current + rights[-1]
    quarter = rows_own.shape[0]
    rows_far = swapped(jnp.concatenate([rows_far, rows_near[quarter:]]), "grp", 2)
    solves, transfer = tree(grams, lefts, rights)
    return basis(solves, rows_own, rows_near, rows_far), transfer


def solution(mesh):
    placed = (
        P("grp", "dev", None, None),
        P("grp", "dev", None, None, None),
        P("grp", "dev", None, None, None),
        P("grp", "dev", None, None),
        P("grp", "dev", None),
    )
    return jax.shard_map(
        on_device,
        mesh=mesh,
        in_specs=placed,
        out_specs=(P("dev", "grp", None), P("dev", None, None)),
        check_vma=False,
    )
```

```python
import functools

import jax
import jax.numpy as jnp
from jax import lax
from jax.experimental import pallas as pl
from jax.experimental.pallas import tpu as pltpu
from jax.sharding import PartitionSpec as P


f32 = jnp.float32
bf16 = jnp.bfloat16
VM = pl.BlockSpec(memory_space=pltpu.VMEM)
SM = pl.BlockSpec(memory_space=pltpu.SMEM)


def swapped(value, axis, mask):
    pairs = [(source, source ^ mask) for source in range(lax.axis_size(axis))]
    return lax.ppermute(value, axis, pairs)


def split(x):
    high = x.astype(bf16)
    low = (x - high.astype(f32)).astype(bf16)
    return high, low


def dot_full(x, y, dims):
    return lax.dot_general(
        x, y, (dims, ((), ())), precision=lax.Precision.HIGHEST, preferred_element_type=f32
    )


def table_kernel(order, unit, n_local, cols_ref, ranks_ref, v_ref, slot_ref, held_ref, sem):
    copy = pltpu.make_async_copy(v_ref, held_ref, sem)
    copy.start()
    n_leaf, _, n_blocks = cols_ref.shape
    depth, clusters = slot_ref.shape
    position = lax.broadcasted_iota(jnp.int32, (clusters, 1), 0)
    names = jnp.zeros((clusters, 1), jnp.int32)
    for at, cluster in enumerate(order):
        names = jnp.where(position == at, cluster, names)
    names = jnp.bitwise_xor(names, lax.axis_index("dev") * n_local)
    ones = jnp.ones((n_blocks, n_blocks), bf16)
    si = lax.broadcasted_iota(jnp.int32, (n_blocks, n_blocks), 0)
    li = lax.broadcasted_iota(jnp.int32, (n_blocks, n_blocks), 1)
    before = jnp.where(si < li, 1.0, 0.0).astype(bf16)
    number = lax.broadcasted_iota(jnp.int32, (depth, n_blocks), 1).astype(f32)
    level = lax.broadcasted_iota(jnp.int32, (depth, n_blocks), 0).astype(f32)
    offset = jnp.zeros((clusters, n_blocks), f32)
    index = jnp.zeros((depth, clusters), f32)
    rank = jnp.zeros((depth, clusters), f32)
    used = jnp.zeros((depth, clusters), f32)
    for c in range(n_leaf):
        named = jnp.where(cols_ref[c] == names, 1.0, 0.0)
        named_low = named.astype(bf16)

        def listed(x, named_low=named_low):
            return lax.dot_general(
                x.astype(bf16), named_low, (((1,), (1,)), ((), ())), preferred_element_type=f32
            )

        ahead = offset + jnp.dot(named_low, before, preferred_element_type=f32)
        place = jnp.sum(named * ahead, axis=0, keepdims=True)
        mark = jnp.where(place == level, 1.0, 0.0)
        here = listed(mark)
        index = index + listed(mark * number) + here * float(c * n_blocks)
        rank = rank + listed(mark * ranks_ref[c : c + 1, :].astype(f32))
        used = used + here
        offset = offset + jnp.dot(named_low, ones, preferred_element_type=f32)
    index = jnp.where(used > 0.5, index, float(n_leaf * n_blocks))
    slot_ref[...] = index.astype(jnp.int32) * unit + rank.astype(jnp.int32)
    copy.wait()


def slot_table(order, cols, ranks, v, depth, unit, n_local):
    return pl.pallas_call(
        functools.partial(table_kernel, order, unit, n_local),
        out_shape=(
            jax.ShapeDtypeStruct((depth, len(order)), jnp.int32),
            jax.ShapeDtypeStruct(v.shape, f32),
        ),
        in_specs=[VM, VM, pl.BlockSpec(memory_space=pltpu.HBM)],
        out_specs=(VM, VM),
        scratch_shapes=[pltpu.SemaphoreType.DMA],
        compiler_params=pltpu.CompilerParams(vmem_limit_bytes=38 << 20),
        cost_estimate=pl.CostEstimate(flops=0, bytes_accessed=24 << 20, transcendentals=0),
        name="slots",
    )(cols, ranks, v)


def coeff_kernel(most, start, unit, n_pieces, part, parts, *refs):
    slot_ref, v_ref = refs[:2]
    pieces = refs[2 : 2 + n_pieces]
    if part is None:
        c_ref, w_ref = refs[-2:]
    else:
        u_ref = refs[2 + n_pieces]
        c_ref, held_ref, w_ref, sem = refs[-4:]
        length = u_ref.shape[0] // parts
        stretch = pl.ds(part * length, length)
        copy = pltpu.make_async_copy(u_ref.at[stretch], held_ref.at[stretch], sem)
        copy.start()
    p = pieces[0].shape[2]
    n_all, k, _ = v_ref.shape
    at = 0
    for piece in pieces:
        for q in range(piece.shape[0]):
            high, low = split(piece[q])
            w_ref[at, :, :p] = high
            w_ref[at, :, p:] = low
            at += 1
    sub = lax.broadcasted_iota(jnp.int32, (k, p), 0)

    def body(j, _):
        highs, lows, ids, kept = [], [], [], []
        for n in range(most):
            entry = slot_ref[n, start + j]
            b = entry // unit
            ids.append(b)
            kept.append(sub < entry % unit)
            high, low = split(v_ref[jnp.minimum(b, n_all - 1)])
            highs.append(high)
            lows.append(low)
        w = w_ref[j]
        both = jnp.dot(jnp.concatenate(highs, 0), w, preferred_element_type=f32)
        both = both + jnp.dot(jnp.concatenate(lows, 0), w, preferred_element_type=f32)
        total = both[:, :p] + both[:, p:]
        for n in range(most):
            c_ref[ids[n]] = jnp.where(kept[n], total[n * k : (n + 1) * k], 0.0)
        return 0

    lax.fori_loop(0, at, body, 0, unroll=4)
    if part is not None:
        copy.wait()


def coefficients(slots, v, pieces, start, most, unit, before, u=None, held_u=None, part=None, parts=1):
    n_all, k, rows = v.shape
    p = pieces[0].shape[2]
    held = sum(piece.shape[0] for piece in pieces)
    args = [slots, v, *pieces]
    specs = [SM] + [VM] * (1 + len(pieces))
    shapes = [jax.ShapeDtypeStruct((n_all + 1, k, p), f32)]
    scratch = [pltpu.VMEM((held, rows, 2 * p), bf16)]
    copying = part is not None
    if copying:
        args.append(u)
        specs.append(pl.BlockSpec(memory_space=pltpu.HBM))
        shapes.append(jax.ShapeDtypeStruct(u.shape, f32))
        scratch.append(pltpu.SemaphoreType.DMA)
    aliases = {}
    for output, value in enumerate((before, held_u)):
        if value is not None:
            aliases[len(args)] = output
            args.append(value)
            specs.append(VM)
    out = pl.pallas_call(
        functools.partial(coeff_kernel, most, start, unit, len(pieces), part, parts),
        out_shape=tuple(shapes),
        in_specs=specs,
        out_specs=(VM,) * len(shapes),
        scratch_shapes=scratch,
        input_output_aliases=aliases,
        compiler_params=pltpu.CompilerParams(vmem_limit_bytes=(20 if copying else 12) << 20),
        cost_estimate=pl.CostEstimate(
            flops=0, bytes_accessed=held * 192 << 10, transcendentals=0
        ),
        name="coeff",
    )(*args)
    return out if copying else (out[0], None)


def sketch_kernel(m, n_blocks, c_ref, u_ref, o_ref):
    p, rows = o_ref.shape
    k = u_ref.shape[1]
    step = rows // k
    leaf = jnp.bitwise_xor(lax.axis_index("grp"), m)
    total = jnp.zeros((p, rows), f32)
    for q in range(n_blocks // step):
        at = pl.ds(leaf * n_blocks + q * step, step)
        high, low = split(c_ref[at].reshape(rows, p).T)
        u_high, u_low = split(u_ref[at].reshape(rows, rows))
        total = total + jnp.dot(high, u_high, preferred_element_type=f32)
        total = total + jnp.dot(low, u_high, preferred_element_type=f32)
        total = total + jnp.dot(high, u_low, preferred_element_type=f32)
    o_ref[...] = total


def sketch(coeff, u, m, n_blocks):
    k, rows = u.shape[1:]
    p = coeff.shape[2]
    return pl.pallas_call(
        functools.partial(sketch_kernel, m, n_blocks),
        out_shape=jax.ShapeDtypeStruct((p, rows), f32),
        in_specs=[VM, VM],
        out_specs=VM,
        compiler_params=pltpu.CompilerParams(vmem_limit_bytes=8 << 20),
        cost_estimate=pl.CostEstimate(
            flops=n_blocks * k * rows * p * 6, bytes_accessed=1 << 20, transcendentals=0
        ),
        name="sketch",
    )(coeff, u)


def pack(gram):
    p = gram.shape[0]
    block = p // 4
    half = block // 2
    lane = lax.broadcasted_iota(jnp.int32, (block, p), 1)
    second = jnp.where(lane < block, pltpu.roll(gram[3 * block :], block, 1), gram[block : 2 * block])
    third = gram[2 * block : 3 * block]
    third = jnp.where(lane[:half] < 2 * block, pltpu.roll(third[half:], 2 * block, 1), third[:half])
    return jnp.concatenate([gram[:block], second, third], axis=0)


def unpack_to(ref, index, packed):
    p = packed.shape[1]
    block = p // 4
    half = block // 2
    third = packed[2 * block :]
    ref[index, : 2 * block + half] = packed
    ref[index, 2 * block + half : 3 * block] = pltpu.roll(third, 2 * block, 1)
    ref[index, 3 * block :] = pltpu.roll(packed[block : 2 * block], 3 * block, 1)


def gram_kernel(n_terms, *refs):
    terms = refs[:n_terms]
    gram_ref, near_ref, far_ref, keep_ref, hold_ref = refs[n_terms:]
    total = terms[0][...]
    for term in terms[1:]:
        total = total + term[...]
    gram_ref[...] = pack(dot_full(total, total, ((1,), (1,))))
    hold_ref[...] = total.T
    quarter = keep_ref.shape[0]

    def rows_of(m):
        at = pl.multiple_of(jnp.bitwise_xor(lax.axis_index("grp"), m) * quarter, quarter)
        return hold_ref[pl.ds(at, quarter), :]

    near_ref[:quarter] = rows_of(1)
    near_ref[quarter:] = rows_of(3)
    far_ref[...] = rows_of(2)
    keep_ref[...] = rows_of(0)


def gram_of(terms, n_grp):
    p, rows = terms[0].shape
    quarter = rows // n_grp
    return pl.pallas_call(
        functools.partial(gram_kernel, len(terms)),
        out_shape=tuple(
            jax.ShapeDtypeStruct((height, p), f32)
            for height in (p // 8 * 5, 2 * quarter, quarter, quarter)
        ),
        in_specs=[VM] * len(terms),
        out_specs=(VM, VM, VM, VM),
        scratch_shapes=[pltpu.VMEM((rows, p), f32)],
        compiler_params=pltpu.CompilerParams(vmem_limit_bytes=8 << 20),
        name="gram",
    )(*terms)


def split3(x):
    high = x.astype(bf16)
    rest = x - high.astype(f32)
    mid = rest.astype(bf16)
    return high, mid, (rest - mid.astype(f32)).astype(bf16)


def factor(m_ref, panel, group):
    count, p, _ = m_ref.shape
    lane = lax.broadcasted_iota(jnp.int32, (1, 1, p), 2)
    sub8 = lax.broadcasted_iota(jnp.int32, (1, 8, p), 1)
    n_tiles = panel // 8
    for base in range(0, p, panel):
        after = base + panel
        x = [m_ref[:, base + 8 * i : base + 8 * i + 8, :] for i in range(n_tiles)]
        for t0 in range(0, panel, group):
            i0 = t0 // 8
            tiles = range(i0, n_tiles)
            columns = []
            for s in range(t0, t0 + group):
                k = base + s
                columns.append([jnp.broadcast_to(x[i][:, :, k : k + 1], x[i].shape) for i in tiles])
            for t in range(group):
                ts = (t0 + t) % 8
                hit = lane == base + t0 + t
                scale = lax.rsqrt(columns[t][0][:, ts : ts + 1, :])
                parts = [column * scale for column in columns[t]]
                for s in range(t + 1, group):
                    ss = (t0 + s) % 8
                    weight = parts[0][:, ss : ss + 1, :]
                    columns[s] = [c - part * weight for c, part in zip(columns[s], parts)]
                row = jnp.where(hit, 1.0, x[i0][:, ts : ts + 1, :]) * scale
                for i in tiles:
                    new = jnp.where(hit, 0.0, x[i]) - parts[i - i0] * row
                    if i == i0:
                        new = jnp.where(sub8 < ts, x[i], jnp.where(sub8 == ts, row, new))
                    x[i] = new
        for i in range(n_tiles):
            m_ref[:, base + 8 * i : base + 8 * i + 8, :] = x[i]
        if after < p:
            for b in range(count):
                block = m_ref[b, base:after, :]
                si = lax.broadcasted_iota(jnp.int32, block.shape, 0)
                li = lax.broadcasted_iota(jnp.int32, block.shape, 1)
                right = jnp.where((li < after) & (li - base > si), 0.0, block)
                high, mid, low = split3(block)
                r_high, r_mid, r_low = split3(right)
                zero = jnp.zeros_like(r_low)
                lhs = jnp.concatenate([high, mid, low, high], axis=0).T[after:, :]
                first = jnp.concatenate([r_high, r_high, r_high, r_low], axis=0)
                second = jnp.concatenate([r_mid, r_mid, zero, zero], axis=0)
                rhs = jnp.concatenate([first, second], axis=1)
                both = jnp.dot(lhs, rhs, preferred_element_type=f32)
                change = both[:, :p] + both[:, p:]
                old = m_ref[b, after:, :]
                lj = lax.broadcasted_iota(jnp.int32, old.shape, 1)
                old = jnp.where((lj >= base) & (lj < after), 0.0, old)
                m_ref[b, after:, :] = old - change


def applied(x, solve):
    p = x.shape[1]
    high, low = split(x)
    dims = (((1,), (1,)), ((), ()))
    both = lax.dot_general(high, solve, dims, preferred_element_type=f32)
    both = both + lax.dot_general(low, solve, dims, preferred_element_type=f32)
    return both[:, :p] + both[:, p:]


def tree_kernel(panel, group, n_leaf, n_levels, *refs):
    grams = refs[:n_leaf]
    lefts = refs[n_leaf : n_leaf + n_levels]
    rights = refs[n_leaf + n_levels : n_leaf + 2 * n_levels]
    solve_ref, tr_ref, m_ref, pick_ref = refs[n_leaf + 2 * n_levels :]
    p = m_ref.shape[1]
    own = lax.axis_index("grp")
    device = lax.axis_index("dev")
    for m in range(n_leaf):
        unpack_to(m_ref, jnp.bitwise_xor(own, m), grams[m][...])
    m_ref[4] = m_ref[0] + m_ref[1]
    m_ref[5] = m_ref[2] + m_ref[3]
    m_ref[6] = m_ref[4] + m_ref[5]
    pick_ref[0] = grams[0][...]
    pick_ref[1] = grams[1][...]
    for level in range(n_levels):

        @pl.when(device % 2 ** (level + 1) == 2**level - 1)
        def _(level=level):
            pick_ref[0] = lefts[level][...]
            pick_ref[1] = rights[level][...]

    unpack_to(m_ref, 7, pick_ref[0])
    unpack_to(m_ref, 8, pick_ref[1])
    m_ref[9] = m_ref[7] + m_ref[8]
    factor(m_ref, panel, group)
    ri = lax.broadcasted_iota(jnp.int32, (p, p), 0)
    ci = lax.broadcasted_iota(jnp.int32, (p, p), 1)

    def inverse(b):
        return jnp.concatenate(split(jnp.where(ci <= ri, m_ref[b], 0.0)), axis=0)

    def upper(b):
        whole = m_ref[b]
        return jnp.where(ci > ri, whole, jnp.where(ci == ri, 1.0 / whole, 0.0))

    for leaf in range(n_leaf):
        solve_ref[leaf] = inverse(leaf)
    keep = device != lax.axis_size("dev") - 1
    for q, (a, b, node) in enumerate(((0, 1, 4), (2, 3, 5), (4, 5, 6), (7, 8, 9))):
        made = applied(jnp.concatenate([upper(a), upper(b)], axis=0), inverse(node))
        tr_ref[q] = jnp.where(keep, made, 0.0) if q == 3 else made


def tree(grams, lefts, rights, group=4):
    p = grams[0].shape[1]
    panel = p // 4
    n_leaf = len(grams)
    arrays = [*grams, *lefts, *rights]
    return pl.pallas_call(
        functools.partial(tree_kernel, panel, group, n_leaf, len(lefts)),
        out_shape=(
            jax.ShapeDtypeStruct((n_leaf, 2 * p, p), bf16),
            jax.ShapeDtypeStruct((4, 2 * p, p), f32),
        ),
        in_specs=[VM] * len(arrays),
        out_specs=(VM, VM),
        scratch_shapes=[pltpu.VMEM((10, p, p), f32), pltpu.VMEM((2, *grams[0].shape), f32)],
        compiler_params=pltpu.CompilerParams(vmem_limit_bytes=16 << 20),
        cost_estimate=pl.CostEstimate(flops=0, bytes_accessed=24 << 20, transcendentals=0),
        name="tree",
    )(*arrays)


def basis_kernel(solve_ref, own_ref, near_ref, far_ref, basis_ref):
    own = lax.axis_index("grp")
    quarter = own_ref.shape[0]
    rows = (own_ref[...], near_ref[:quarter], far_ref[:quarter], far_ref[quarter:])
    for m, value in enumerate(rows):
        leaf = jnp.bitwise_xor(own, m)
        basis_ref[leaf] = applied(value, solve_ref[leaf])


def basis(solves, own, near, far):
    n_leaf = solves.shape[0]
    quarter, p = own.shape
    return pl.pallas_call(
        basis_kernel,
        out_shape=jax.ShapeDtypeStruct((n_leaf, quarter, p), f32),
        in_specs=[VM] * 4,
        out_specs=VM,
        compiler_params=pltpu.CompilerParams(vmem_limit_bytes=8 << 20),
        name="basis",
    )(solves, own, near, far)


def gathered(omega, dev_count):
    n_local = omega.shape[0]
    half = n_local // 2
    masks = [2**bit for bit in range(1, dev_count.bit_length() - 1)]
    waves = {}
    for order, first in ((masks, 0), (masks[::-1], half)):
        held = [(0, 0, omega[first : first + half])]
        for place, mask in enumerate(order):
            new = [
                (max(level, place) + (seen > 0), seen ^ mask, value) for level, seen, value in held
            ]
            for at, (level, seen, value) in enumerate(new):
                new[at] = (level, seen, swapped(value, "dev", mask))
            for level, seen, value in new:
                waves.setdefault(level, []).append((seen, first, value))
            held = held + new
    other = swapped(omega, "dev", 1)
    order = [mask * n_local + q for mask in (0, 1) for q in range(n_local)]
    groups = [[omega[:half], omega[half:], other]]
    for level in sorted(waves):
        wave = waves[level]
        for flip in (0, 1):
            for seen, first, value in wave:
                order.extend((seen ^ flip) * n_local + first + q for q in range(half))

        values = [value for _, _, value in wave]
        others = [swapped(value, "dev", 1) for value in values]
        if level == 0:
            groups.append(values + others)
        else:
            groups.extend([values, others])
    return groups, order


def on_device(omega, u_factor, v_factor, columns, ranks):
    n_local, n_blocks = u_factor.shape[1:3]
    leaf_rows, width = u_factor.shape[3:]
    dev_count = lax.axis_size("dev")
    grp_count = lax.axis_size("grp")
    assert n_local == grp_count == 4
    clusters = n_local * dev_count
    most = -(-11 * n_local * n_blocks // (10 * clusters))
    v = jnp.swapaxes(v_factor[0], 2, 3).reshape(n_local * n_blocks, width, leaf_rows)
    u = jnp.swapaxes(u_factor[0], 2, 3).reshape(n_local * n_blocks, width, leaf_rows)
    groups, order = gathered(omega[0], dev_count)
    depth = -(-most // 8) * 8
    unit = 2 * width
    columns = jnp.swapaxes(columns[0], 1, 2)
    slots, v = slot_table(tuple(order), columns, ranks[0], v, depth, unit, n_local)
    coeff = held_u = None
    start = 0
    for index, pieces in enumerate(groups):
        if index < 2:
            copied = (u, held_u, index, 2)
            coeff, held_u = coefficients(slots, v, pieces, start, most, unit, coeff, *copied)
        else:
            coeff, _ = coefficients(slots, v, pieces, start, most, unit, coeff)
        start += sum(piece.shape[0] for piece in pieces)
    made = {}
    for m in (3, 2, 1, 0):
        made[m] = sketch(coeff, held_u, m, n_blocks)
    across = swapped(made[3], "grp", 1)
    across = swapped(made[2] + across, "grp", 2)
    beside = swapped(made[1], "grp", 1)
    gram, rows_near, rows_far, rows_own = gram_of([made[0], beside, across], grp_count)
    near_in = swapped(gram, "grp", 1)
    far_in = swapped(gram, "grp", 2)
    pass_in = swapped(near_in, "grp", 2)
    rows_near = swapped(rows_near, "grp", 1)
    grams = [gram, near_in, far_in, pass_in]
    current = (gram + near_in) + (far_in + pass_in)
    lefts, rights = [], []
    masks = [2**bit for bit in range(dev_count.bit_length() - 1)]
    steps = [masks[:1]] + [masks[at : at + 2] for at in range(1, len(masks), 2)]
    for step in steps:
        first = swapped(current, "dev", step[0])
        wider = [swapped(current, "dev", extra ^ step[1]) for extra in (0, step[0])] if step[1:] else []
        lefts.append(current)
        rights.append(first)
        current = current + first
        if wider:
            lefts.append(current)
            rights.append(wider[0] + wider[1])
            current = current + rights[-1]
    quarter = rows_own.shape[0]
    rows_far = swapped(jnp.concatenate([rows_far, rows_near[quarter:]]), "grp", 2)
    solves, transfer = tree(grams, lefts, rights)
    return basis(solves, rows_own, rows_near, rows_far), transfer


def solution(mesh):
    placed = (
        P("grp", "dev", None, None),
        P("grp", "dev", None, None, None),
        P("grp", "dev", None, None, None),
        P("grp", "dev", None, None),
        P("grp", "dev", None),
    )
    return jax.shard_map(
        on_device,
        mesh=mesh,
        in_specs=placed,
        out_specs=(P("dev", "grp", None), P("dev", None, None)),
        check_vma=False,
    )
```

```python
import functools

import jax
import jax.numpy as jnp
from jax import lax
from jax.experimental import pallas as pl
from jax.experimental.pallas import tpu as pltpu
from jax.sharding import PartitionSpec as P


f32 = jnp.float32
bf16 = jnp.bfloat16
VM = pl.BlockSpec(memory_space=pltpu.VMEM)
SM = pl.BlockSpec(memory_space=pltpu.SMEM)


def swapped(value, axis, mask):
    pairs = [(source, source ^ mask) for source in range(lax.axis_size(axis))]
    return lax.ppermute(value, axis, pairs)


def split(x):
    high = x.astype(bf16)
    low = (x - high.astype(f32)).astype(bf16)
    return high, low


def dot_full(x, y, dims):
    return lax.dot_general(
        x, y, (dims, ((), ())), precision=lax.Precision.HIGHEST, preferred_element_type=f32
    )


def in_hbm(x):
    return pltpu.with_memory_space_constraint(x, pltpu.HBM)


def table_kernel(order, unit, n_local, part, cols_ref, ranks_ref, v_ref, u_ref, *refs):
    slot_ref, held_ref, held_u_ref, sem, sem_u = refs
    copy = pltpu.make_async_copy(v_ref, held_ref, sem)
    copy.start()
    stretch = pl.ds(*part)
    copy_u = pltpu.make_async_copy(u_ref.at[stretch], held_u_ref.at[stretch], sem_u)
    copy_u.start()
    n_leaf, _, n_blocks = cols_ref.shape
    depth, clusters = slot_ref.shape
    position = lax.broadcasted_iota(jnp.int32, (clusters, 1), 0)
    names = jnp.zeros((clusters, 1), jnp.int32)
    for at, cluster in enumerate(order):
        names = jnp.where(position == at, cluster, names)
    names = jnp.bitwise_xor(names, lax.axis_index("dev") * n_local)
    ones = jnp.ones((n_blocks, n_blocks), bf16)
    si = lax.broadcasted_iota(jnp.int32, (n_blocks, n_blocks), 0)
    li = lax.broadcasted_iota(jnp.int32, (n_blocks, n_blocks), 1)
    before = jnp.where(si < li, 1.0, 0.0).astype(bf16)
    number = lax.broadcasted_iota(jnp.int32, (depth, n_blocks), 1).astype(f32)
    level = lax.broadcasted_iota(jnp.int32, (depth, n_blocks), 0).astype(f32)
    offset = jnp.zeros((clusters, n_blocks), f32)
    index = jnp.zeros((depth, clusters), f32)
    rank = jnp.zeros((depth, clusters), f32)
    used = jnp.zeros((depth, clusters), f32)
    for c in range(n_leaf):
        named = jnp.where(cols_ref[c] == names, 1.0, 0.0)
        named_low = named.astype(bf16)

        def listed(x, named_low=named_low):
            return lax.dot_general(
                x.astype(bf16), named_low, (((1,), (1,)), ((), ())), preferred_element_type=f32
            )

        ahead = offset + jnp.dot(named_low, before, preferred_element_type=f32)
        place = jnp.sum(named * ahead, axis=0, keepdims=True)
        mark = jnp.where(place == level, 1.0, 0.0)
        here = listed(mark)
        index = index + listed(mark * number) + here * float(c * n_blocks)
        rank = rank + listed(mark * ranks_ref[c : c + 1, :].astype(f32))
        used = used + here
        offset = offset + jnp.dot(named_low, ones, preferred_element_type=f32)
    index = jnp.where(used > 0.5, index, float(n_leaf * n_blocks))
    slot_ref[...] = index.astype(jnp.int32) * unit + rank.astype(jnp.int32)
    copy.wait()
    copy_u.wait()


def slot_table(order, cols, ranks, v, u, part, depth, unit, n_local):
    return pl.pallas_call(
        functools.partial(table_kernel, order, unit, n_local, part),
        out_shape=(
            jax.ShapeDtypeStruct((depth, len(order)), jnp.int32),
            jax.ShapeDtypeStruct(v.shape, f32),
            jax.ShapeDtypeStruct(u.shape, f32),
        ),
        in_specs=[VM, VM] + [pl.BlockSpec(memory_space=pltpu.HBM)] * 2,
        out_specs=(VM, VM, VM),
        scratch_shapes=[pltpu.SemaphoreType.DMA, pltpu.SemaphoreType.DMA],
        compiler_params=pltpu.CompilerParams(vmem_limit_bytes=4 << 20),
        cost_estimate=pl.CostEstimate(flops=0, bytes_accessed=24 << 20, transcendentals=0),
        name="slots",
    )(cols, ranks, in_hbm(v), in_hbm(u))


def coeff_kernel(most, start, unit, n_pieces, part, *refs):
    slot_ref, v_ref = refs[:2]
    pieces = refs[2 : 2 + n_pieces]
    if part is None:
        c_ref = refs[-1]
    else:
        u_ref = refs[2 + n_pieces]
        c_ref, held_ref, sem = refs[-3:]
        stretch = pl.ds(*part)
        copy = pltpu.make_async_copy(u_ref.at[stretch], held_ref.at[stretch], sem)
        copy.start()
    p = pieces[0].shape[2]
    n_all, k, _ = v_ref.shape
    sub = lax.broadcasted_iota(jnp.int32, (k, p), 0)
    at = start
    for piece in pieces:
        for q in range(piece.shape[0]):
            w = jnp.concatenate(split(piece[q]), axis=1)
            highs, lows, ids, kept = [], [], [], []
            for n in range(most):
                entry = slot_ref[n, at]
                b = entry // unit
                ids.append(b)
                kept.append(sub < entry % unit)
                high, low = split(v_ref[jnp.minimum(b, n_all - 1)])
                highs.append(high)
                lows.append(low)
            both = jnp.dot(jnp.concatenate(highs, 0), w, preferred_element_type=f32)
            both = both + jnp.dot(jnp.concatenate(lows, 0), w, preferred_element_type=f32)
            total = both[:, :p] + both[:, p:]
            for n in range(most):
                c_ref[ids[n]] = jnp.where(kept[n], total[n * k : (n + 1) * k], 0.0)
            at += 1
    if part is not None:
        copy.wait()


def coefficients(slots, v, pieces, start, most, unit, before, u=None, held_u=None, part=None):
    n_all, k, _ = v.shape
    p = pieces[0].shape[2]
    held = sum(piece.shape[0] for piece in pieces)
    args = [slots, v, *pieces]
    specs = [SM] + [VM] * (1 + len(pieces))
    shapes = [jax.ShapeDtypeStruct((n_all + 1, k, p), f32)]
    scratch = []
    copying = part is not None
    if copying:
        args.append(in_hbm(u))
        specs.append(pl.BlockSpec(memory_space=pltpu.HBM))
        shapes.append(jax.ShapeDtypeStruct(u.shape, f32))
        scratch.append(pltpu.SemaphoreType.DMA)
    aliases = {}
    for output, value in enumerate((before, held_u)):
        if value is not None:
            aliases[len(args)] = output
            args.append(value)
            specs.append(VM)
    out = pl.pallas_call(
        functools.partial(coeff_kernel, most, start, unit, len(pieces), part),
        out_shape=tuple(shapes),
        in_specs=specs,
        out_specs=(VM,) * len(shapes),
        scratch_shapes=scratch,
        input_output_aliases=aliases,
        compiler_params=pltpu.CompilerParams(vmem_limit_bytes=12 << 20),
        cost_estimate=pl.CostEstimate(
            flops=0, bytes_accessed=held * 192 << 10, transcendentals=0
        ),
        name="coeff",
    )(*args)
    return out if copying else (out[0], None)


def sketch_kernel(m, n_blocks, c_ref, u_ref, o_ref):
    p, rows = o_ref.shape
    k = u_ref.shape[1]
    step = rows // k
    leaf = jnp.bitwise_xor(lax.axis_index("grp"), m)
    total = jnp.zeros((p, rows), f32)
    for q in range(n_blocks // step):
        at = pl.ds(leaf * n_blocks + q * step, step)
        high, low = split(c_ref[at].reshape(rows, p).T)
        u_high, u_low = split(u_ref[at].reshape(rows, rows))
        total = total + jnp.dot(high, u_high, preferred_element_type=f32)
        total = total + jnp.dot(low, u_high, preferred_element_type=f32)
        total = total + jnp.dot(high, u_low, preferred_element_type=f32)
    o_ref[...] = total


def sketch(coeff, u, m, n_blocks):
    k, rows = u.shape[1:]
    p = coeff.shape[2]
    return pl.pallas_call(
        functools.partial(sketch_kernel, m, n_blocks),
        out_shape=jax.ShapeDtypeStruct((p, rows), f32),
        in_specs=[VM, VM],
        out_specs=VM,
        compiler_params=pltpu.CompilerParams(vmem_limit_bytes=8 << 20),
        cost_estimate=pl.CostEstimate(
            flops=n_blocks * k * rows * p * 6, bytes_accessed=1 << 20, transcendentals=0
        ),
        name="sketch",
    )(coeff, u)


def pack(gram):
    p = gram.shape[0]
    block = p // 4
    half = block // 2
    lane = lax.broadcasted_iota(jnp.int32, (block, p), 1)
    second = jnp.where(lane < block, pltpu.roll(gram[3 * block :], block, 1), gram[block : 2 * block])
    third = gram[2 * block : 3 * block]
    third = jnp.where(lane[:half] < 2 * block, pltpu.roll(third[half:], 2 * block, 1), third[:half])
    return jnp.concatenate([gram[:block], second, third], axis=0)


def unpack_to(ref, index, packed):
    p = packed.shape[1]
    block = p // 4
    half = block // 2
    third = packed[2 * block :]
    ref[index, : 2 * block + half] = packed
    ref[index, 2 * block + half : 3 * block] = pltpu.roll(third, 2 * block, 1)
    ref[index, 3 * block :] = pltpu.roll(packed[block : 2 * block], 3 * block, 1)


def gram_kernel(n_terms, *refs):
    terms = refs[:n_terms]
    gram_ref, near_ref, far_ref, keep_ref, hold_ref = refs[n_terms:]
    total = terms[0][...]
    for term in terms[1:]:
        total = total + term[...]
    gram_ref[...] = pack(dot_full(total, total, ((1,), (1,))))
    hold_ref[...] = total.T
    quarter = keep_ref.shape[0]

    def rows_of(m):
        at = pl.multiple_of(jnp.bitwise_xor(lax.axis_index("grp"), m) * quarter, quarter)
        return hold_ref[pl.ds(at, quarter), :]

    near_ref[:quarter] = rows_of(1)
    near_ref[quarter:] = rows_of(3)
    far_ref[...] = rows_of(2)
    keep_ref[...] = rows_of(0)


def gram_of(terms, n_grp):
    p, rows = terms[0].shape
    quarter = rows // n_grp
    return pl.pallas_call(
        functools.partial(gram_kernel, len(terms)),
        out_shape=tuple(
            jax.ShapeDtypeStruct((height, p), f32)
            for height in (p // 8 * 5, 2 * quarter, quarter, quarter)
        ),
        in_specs=[VM] * len(terms),
        out_specs=(VM, VM, VM, VM),
        scratch_shapes=[pltpu.VMEM((rows, p), f32)],
        compiler_params=pltpu.CompilerParams(vmem_limit_bytes=8 << 20),
        name="gram",
    )(*terms)


def split3(x):
    high = x.astype(bf16)
    rest = x - high.astype(f32)
    mid = rest.astype(bf16)
    return high, mid, (rest - mid.astype(f32)).astype(bf16)


def factor(m_ref, panel, group):
    count, p, _ = m_ref.shape
    lane = lax.broadcasted_iota(jnp.int32, (1, 1, p), 2)
    sub8 = lax.broadcasted_iota(jnp.int32, (1, 8, p), 1)
    n_tiles = panel // 8
    for base in range(0, p, panel):
        after = base + panel
        x = [m_ref[:, base + 8 * i : base + 8 * i + 8, :] for i in range(n_tiles)]
        for t0 in range(0, panel, group):
            i0 = t0 // 8
            tiles = range(i0, n_tiles)
            columns = []
            for s in range(t0, t0 + group):
                k = base + s
                columns.append([jnp.broadcast_to(x[i][:, :, k : k + 1], x[i].shape) for i in tiles])
            for t in range(group):
                ts = (t0 + t) % 8
                hit = lane == base + t0 + t
                scale = lax.rsqrt(columns[t][0][:, ts : ts + 1, :])
                parts = [column * scale for column in columns[t]]
                for s in range(t + 1, group):
                    ss = (t0 + s) % 8
                    weight = parts[0][:, ss : ss + 1, :]
                    columns[s] = [c - part * weight for c, part in zip(columns[s], parts)]
                row = jnp.where(hit, 1.0, x[i0][:, ts : ts + 1, :]) * scale
                for i in tiles:
                    new = jnp.where(hit, 0.0, x[i]) - parts[i - i0] * row
                    if i == i0:
                        new = jnp.where(sub8 < ts, x[i], jnp.where(sub8 == ts, row, new))
                    x[i] = new
        for i in range(n_tiles):
            m_ref[:, base + 8 * i : base + 8 * i + 8, :] = x[i]
        if after < p:
            for b in range(count):
                block = m_ref[b, base:after, :]
                si = lax.broadcasted_iota(jnp.int32, block.shape, 0)
                li = lax.broadcasted_iota(jnp.int32, block.shape, 1)
                right = jnp.where((li < after) & (li - base > si), 0.0, block)
                high, mid, low = split3(block)
                r_high, r_mid, r_low = split3(right)
                zero = jnp.zeros_like(r_low)
                lhs = jnp.concatenate([high, mid, low, high], axis=0).T[after:, :]
                first = jnp.concatenate([r_high, r_high, r_high, r_low], axis=0)
                second = jnp.concatenate([r_mid, r_mid, zero, zero], axis=0)
                rhs = jnp.concatenate([first, second], axis=1)
                both = jnp.dot(lhs, rhs, preferred_element_type=f32)
                change = both[:, :p] + both[:, p:]
                old = m_ref[b, after:, :]
                lj = lax.broadcasted_iota(jnp.int32, old.shape, 1)
                old = jnp.where((lj >= base) & (lj < after), 0.0, old)
                m_ref[b, after:, :] = old - change


def applied(x, solve):
    p = x.shape[1]
    high, low = split(x)
    dims = (((1,), (1,)), ((), ()))
    both = lax.dot_general(high, solve, dims, preferred_element_type=f32)
    both = both + lax.dot_general(low, solve, dims, preferred_element_type=f32)
    return both[:, :p] + both[:, p:]


def tree_kernel(panel, group, n_leaf, n_levels, *refs):
    grams = refs[:n_leaf]
    lefts = refs[n_leaf : n_leaf + n_levels]
    rights = refs[n_leaf + n_levels : n_leaf + 2 * n_levels]
    solve_ref, tr_ref, m_ref, pick_ref = refs[n_leaf + 2 * n_levels :]
    p = m_ref.shape[1]
    own = lax.axis_index("grp")
    device = lax.axis_index("dev")
    for m in range(n_leaf):
        unpack_to(m_ref, jnp.bitwise_xor(own, m), grams[m][...])
    m_ref[4] = m_ref[0] + m_ref[1]
    m_ref[5] = m_ref[2] + m_ref[3]
    m_ref[6] = m_ref[4] + m_ref[5]
    pick_ref[0] = grams[0][...]
    pick_ref[1] = grams[1][...]
    for level in range(n_levels):

        @pl.when(device % 2 ** (level + 1) == 2**level - 1)
        def _(level=level):
            pick_ref[0] = lefts[level][...]
            pick_ref[1] = rights[level][...]

    unpack_to(m_ref, 7, pick_ref[0])
    unpack_to(m_ref, 8, pick_ref[1])
    m_ref[9] = m_ref[7] + m_ref[8]
    factor(m_ref, panel, group)
    ri = lax.broadcasted_iota(jnp.int32, (p, p), 0)
    ci = lax.broadcasted_iota(jnp.int32, (p, p), 1)

    def inverse(b):
        return jnp.concatenate(split(jnp.where(ci <= ri, m_ref[b], 0.0)), axis=0)

    def upper(b):
        whole = m_ref[b]
        return jnp.where(ci > ri, whole, jnp.where(ci == ri, 1.0 / whole, 0.0))

    for leaf in range(n_leaf):
        solve_ref[leaf] = inverse(leaf)
    keep = device != lax.axis_size("dev") - 1
    for q, (a, b, node) in enumerate(((0, 1, 4), (2, 3, 5), (4, 5, 6), (7, 8, 9))):
        made = applied(jnp.concatenate([upper(a), upper(b)], axis=0), inverse(node))
        tr_ref[q] = jnp.where(keep, made, 0.0) if q == 3 else made


def tree(grams, lefts, rights, group=4):
    p = grams[0].shape[1]
    panel = p // 4
    n_leaf = len(grams)
    arrays = [*grams, *lefts, *rights]
    return pl.pallas_call(
        functools.partial(tree_kernel, panel, group, n_leaf, len(lefts)),
        out_shape=(
            jax.ShapeDtypeStruct((n_leaf, 2 * p, p), bf16),
            jax.ShapeDtypeStruct((4, 2 * p, p), f32),
        ),
        in_specs=[VM] * len(arrays),
        out_specs=(VM, VM),
        scratch_shapes=[pltpu.VMEM((10, p, p), f32), pltpu.VMEM((2, *grams[0].shape), f32)],
        compiler_params=pltpu.CompilerParams(vmem_limit_bytes=16 << 20),
        cost_estimate=pl.CostEstimate(flops=0, bytes_accessed=24 << 20, transcendentals=0),
        name="tree",
    )(*arrays)


def basis_kernel(solve_ref, own_ref, near_ref, far_ref, basis_ref):
    own = lax.axis_index("grp")
    quarter = own_ref.shape[0]
    rows = (own_ref[...], near_ref[:quarter], far_ref[:quarter], far_ref[quarter:])
    for m, value in enumerate(rows):
        leaf = jnp.bitwise_xor(own, m)
        basis_ref[leaf] = applied(value, solve_ref[leaf])


def basis(solves, own, near, far):
    n_leaf = solves.shape[0]
    quarter, p = own.shape
    return pl.pallas_call(
        basis_kernel,
        out_shape=jax.ShapeDtypeStruct((n_leaf, quarter, p), f32),
        in_specs=[VM] * 4,
        out_specs=VM,
        compiler_params=pltpu.CompilerParams(vmem_limit_bytes=8 << 20),
        name="basis",
    )(solves, own, near, far)


def gathered(omega, dev_count):
    n_local = omega.shape[0]
    half = n_local // 2
    masks = [2**bit for bit in range(1, dev_count.bit_length() - 1)]
    waves = {}
    for order, first in ((masks, 0), (masks[::-1], half)):
        held = [(0, 0, omega[first : first + half])]
        for place, mask in enumerate(order):
            new = [
                (max(level, place) + (seen > 0), seen ^ mask, value) for level, seen, value in held
            ]
            for at, (level, seen, value) in enumerate(new):
                new[at] = (level, seen, swapped(value, "dev", mask))
            for level, seen, value in new:
                waves.setdefault(level, []).append((seen, first, value))
            held = held + new
    other = swapped(omega, "dev", 1)
    order = [mask * n_local + q for mask in (0, 1) for q in range(n_local)]
    groups = [[omega[:half], omega[half:], other]]
    for level in sorted(waves):
        wave = waves[level]
        for flip in (0, 1):
            for seen, first, value in wave:
                order.extend((seen ^ flip) * n_local + first + q for q in range(half))

        values = [value for _, _, value in wave]
        others = [swapped(value, "dev", 1) for value in values]
        if level == 0:
            groups.append(values + others)
        else:
            groups.extend([values, others])
    return groups, order


def on_device(omega, u_factor, v_factor, columns, ranks):
    n_local, n_blocks = u_factor.shape[1:3]
    leaf_rows, width = u_factor.shape[3:]
    dev_count = lax.axis_size("dev")
    grp_count = lax.axis_size("grp")
    assert n_local == grp_count == 4
    clusters = n_local * dev_count
    most = -(-11 * n_local * n_blocks // (10 * clusters))
    v = jnp.swapaxes(v_factor[0], 2, 3).reshape(n_local * n_blocks, width, leaf_rows)
    u = jnp.swapaxes(u_factor[0], 2, 3).reshape(n_local * n_blocks, width, leaf_rows)
    groups, order = gathered(omega[0], dev_count)
    depth = -(-most // 8) * 8
    unit = 2 * width
    columns = jnp.swapaxes(columns[0], 1, 2)
    cuts = [n_local * n_blocks * tenths // 10 for tenths in (0, 4, 7, 10)]
    parts = [(low, high - low) for low, high in zip(cuts, cuts[1:])]
    slots, v, held_u = slot_table(
        tuple(order), columns, ranks[0], v, u, parts[0], depth, unit, n_local
    )
    coeff = None
    start = 0
    for index, pieces in enumerate(groups):
        if index < 2:
            copied = (u, held_u, parts[index + 1])
            coeff, held_u = coefficients(slots, v, pieces, start, most, unit, coeff, *copied)
        else:
            coeff, _ = coefficients(slots, v, pieces, start, most, unit, coeff)
        start += sum(piece.shape[0] for piece in pieces)
    made = {}
    for m in (3, 2, 1, 0):
        made[m] = sketch(coeff, held_u, m, n_blocks)
    across = swapped(made[3], "grp", 1)
    across = swapped(made[2] + across, "grp", 2)
    beside = swapped(made[1], "grp", 1)
    gram, rows_near, rows_far, rows_own = gram_of([made[0], beside, across], grp_count)
    near_in = swapped(gram, "grp", 1)
    far_in = swapped(gram, "grp", 2)
    pass_in = swapped(near_in, "grp", 2)
    rows_near = swapped(rows_near, "grp", 1)
    grams = [gram, near_in, far_in, pass_in]
    current = (gram + near_in) + (far_in + pass_in)
    lefts, rights = [], []
    masks = [2**bit for bit in range(dev_count.bit_length() - 1)]
    steps = [masks[:1]] + [masks[at : at + 2] for at in range(1, len(masks), 2)]
    for step in steps:
        first = swapped(current, "dev", step[0])
        wider = [swapped(current, "dev", extra ^ step[1]) for extra in (0, step[0])] if step[1:] else []
        lefts.append(current)
        rights.append(first)
        current = current + first
        if wider:
            lefts.append(current)
            rights.append(wider[0] + wider[1])
            current = current + rights[-1]
    quarter = rows_own.shape[0]
    rows_far = swapped(jnp.concatenate([rows_far, rows_near[quarter:]]), "grp", 2)
    solves, transfer = tree(grams, lefts, rights)
    return basis(solves, rows_own, rows_near, rows_far), transfer


def solution(mesh):
    placed = (
        P("grp", "dev", None, None),
        P("grp", "dev", None, None, None),
        P("grp", "dev", None, None, None),
        P("grp", "dev", None, None),
        P("grp", "dev", None),
    )
    return jax.shard_map(
        on_device,
        mesh=mesh,
        in_specs=placed,
        out_specs=(P("dev", "grp", None), P("dev", None, None)),
        check_vma=False,
    )
```

```python
import functools

import jax
import jax.numpy as jnp
from jax import lax
from jax.experimental import pallas as pl
from jax.experimental.pallas import tpu as pltpu
from jax.sharding import PartitionSpec as P


f32 = jnp.float32
bf16 = jnp.bfloat16
VM = pl.BlockSpec(memory_space=pltpu.VMEM)
SM = pl.BlockSpec(memory_space=pltpu.SMEM)


def swapped(value, axis, mask):
    pairs = [(source, source ^ mask) for source in range(lax.axis_size(axis))]
    return lax.ppermute(value, axis, pairs)


def split(x):
    high = x.astype(bf16)
    low = (x - high.astype(f32)).astype(bf16)
    return high, low


def dot_full(x, y, dims):
    return lax.dot_general(
        x, y, (dims, ((), ())), precision=lax.Precision.HIGHEST, preferred_element_type=f32
    )


def in_hbm(x):
    return pltpu.with_memory_space_constraint(x, pltpu.HBM)


def table_kernel(order, unit, n_local, cols_ref, ranks_ref, v_ref, slot_ref, held_ref, sem):
    copy = pltpu.make_async_copy(v_ref, held_ref, sem)
    copy.start()
    n_leaf, _, n_blocks = cols_ref.shape
    depth, clusters = slot_ref.shape
    position = lax.broadcasted_iota(jnp.int32, (clusters, 1), 0)
    names = jnp.zeros((clusters, 1), jnp.int32)
    for at, cluster in enumerate(order):
        names = jnp.where(position == at, cluster, names)
    names = jnp.bitwise_xor(names, lax.axis_index("dev") * n_local)
    ones = jnp.ones((n_blocks, n_blocks), bf16)
    si = lax.broadcasted_iota(jnp.int32, (n_blocks, n_blocks), 0)
    li = lax.broadcasted_iota(jnp.int32, (n_blocks, n_blocks), 1)
    before = jnp.where(si < li, 1.0, 0.0).astype(bf16)
    number = lax.broadcasted_iota(jnp.int32, (depth, n_blocks), 1).astype(f32)
    level = lax.broadcasted_iota(jnp.int32, (depth, n_blocks), 0).astype(f32)
    offset = jnp.zeros((clusters, n_blocks), f32)
    index = jnp.zeros((depth, clusters), f32)
    rank = jnp.zeros((depth, clusters), f32)
    used = jnp.zeros((depth, clusters), f32)
    for c in range(n_leaf):
        named = jnp.where(cols_ref[c] == names, 1.0, 0.0)
        named_low = named.astype(bf16)

        def listed(x, named_low=named_low):
            return lax.dot_general(
                x.astype(bf16), named_low, (((1,), (1,)), ((), ())), preferred_element_type=f32
            )

        ahead = offset + jnp.dot(named_low, before, preferred_element_type=f32)
        place = jnp.sum(named * ahead, axis=0, keepdims=True)
        mark = jnp.where(place == level, 1.0, 0.0)
        here = listed(mark)
        index = index + listed(mark * number) + here * float(c * n_blocks)
        rank = rank + listed(mark * ranks_ref[c : c + 1, :].astype(f32))
        used = used + here
        offset = offset + jnp.dot(named_low, ones, preferred_element_type=f32)
    index = jnp.where(used > 0.5, index, float(n_leaf * n_blocks))
    slot_ref[...] = index.astype(jnp.int32) * unit + rank.astype(jnp.int32)
    copy.wait()


def slot_table(order, cols, ranks, v, depth, unit, n_local):
    return pl.pallas_call(
        functools.partial(table_kernel, order, unit, n_local),
        out_shape=(
            jax.ShapeDtypeStruct((depth, len(order)), jnp.int32),
            jax.ShapeDtypeStruct(v.shape, f32),
        ),
        in_specs=[VM, VM, pl.BlockSpec(memory_space=pltpu.HBM)],
        out_specs=(VM, VM),
        scratch_shapes=[pltpu.SemaphoreType.DMA],
        compiler_params=pltpu.CompilerParams(vmem_limit_bytes=4 << 20),
        cost_estimate=pl.CostEstimate(flops=0, bytes_accessed=24 << 20, transcendentals=0),
        name="slots",
    )(cols, ranks, in_hbm(v))


def coeff_kernel(most, start, unit, n_pieces, *refs):
    slot_ref, v_ref = refs[:2]
    pieces = refs[2 : 2 + n_pieces]
    c_ref, w_ref = refs[-2:]
    p = pieces[0].shape[2]
    n_all, k, _ = v_ref.shape
    at = 0
    for piece in pieces:
        for q in range(piece.shape[0]):
            high, low = split(piece[q])
            w_ref[at, :, :p] = high
            w_ref[at, :, p:] = low
            at += 1
    sub = lax.broadcasted_iota(jnp.int32, (k, p), 0)

    def body(j, _):
        highs, lows, ids, kept = [], [], [], []
        for n in range(most):
            entry = slot_ref[n, start + j]
            b = entry // unit
            ids.append(b)
            kept.append(sub < entry % unit)
            high, low = split(v_ref[jnp.minimum(b, n_all - 1)])
            highs.append(high)
            lows.append(low)
        w = w_ref[j]
        both = jnp.dot(jnp.concatenate(highs, 0), w, preferred_element_type=f32)
        both = both + jnp.dot(jnp.concatenate(lows, 0), w, preferred_element_type=f32)
        total = both[:, :p] + both[:, p:]
        for n in range(most):
            c_ref[ids[n]] = jnp.where(kept[n], total[n * k : (n + 1) * k], 0.0)
        return 0

    lax.fori_loop(0, at, body, 0, unroll=4)


def coefficients(slots, v, pieces, start, most, unit, before, ahead):
    n_all, k, rows = v.shape
    p = pieces[0].shape[2]
    held = sum(piece.shape[0] for piece in pieces)
    args = [slots, v, *pieces] + [value for value in (ahead, before) if value is not None]
    return pl.pallas_call(
        functools.partial(coeff_kernel, most, start, unit, len(pieces)),
        out_shape=jax.ShapeDtypeStruct((n_all + 1, k, p), f32),
        in_specs=[SM] + [VM] * (len(args) - 1),
        out_specs=VM,
        scratch_shapes=[pltpu.VMEM((held, rows, 2 * p), bf16)],
        input_output_aliases={} if before is None else {len(args) - 1: 0},
        compiler_params=pltpu.CompilerParams(vmem_limit_bytes=12 << 20),
        cost_estimate=pl.CostEstimate(
            flops=0, bytes_accessed=held * 192 << 10, transcendentals=0
        ),
        name="coeff",
    )(*args)


def sketch_kernel(m, n_blocks, c_ref, u_ref, o_ref):
    p, rows = o_ref.shape
    k = u_ref.shape[1]
    step = rows // k
    leaf = jnp.bitwise_xor(lax.axis_index("grp"), m)
    total = jnp.zeros((p, rows), f32)
    for q in range(n_blocks // step):
        at = pl.ds(leaf * n_blocks + q * step, step)
        high, low = split(c_ref[at].reshape(rows, p).T)
        u_high, u_low = split(u_ref[at].reshape(rows, rows))
        total = total + jnp.dot(high, u_high, preferred_element_type=f32)
        total = total + jnp.dot(low, u_high, preferred_element_type=f32)
        total = total + jnp.dot(high, u_low, preferred_element_type=f32)
    o_ref[...] = total


def sketch(coeff, u, m, n_blocks):
    k, rows = u.shape[1:]
    p = coeff.shape[2]
    return pl.pallas_call(
        functools.partial(sketch_kernel, m, n_blocks),
        out_shape=jax.ShapeDtypeStruct((p, rows), f32),
        in_specs=[VM, VM],
        out_specs=VM,
        compiler_params=pltpu.CompilerParams(vmem_limit_bytes=8 << 20),
        cost_estimate=pl.CostEstimate(
            flops=n_blocks * k * rows * p * 6, bytes_accessed=1 << 20, transcendentals=0
        ),
        name="sketch",
    )(coeff, u)


def pack(gram):
    p = gram.shape[0]
    block = p // 4
    half = block // 2
    lane = lax.broadcasted_iota(jnp.int32, (block, p), 1)
    second = jnp.where(lane < block, pltpu.roll(gram[3 * block :], block, 1), gram[block : 2 * block])
    third = gram[2 * block : 3 * block]
    third = jnp.where(lane[:half] < 2 * block, pltpu.roll(third[half:], 2 * block, 1), third[:half])
    return jnp.concatenate([gram[:block], second, third], axis=0)


def unpack_to(ref, index, packed):
    p = packed.shape[1]
    block = p // 4
    half = block // 2
    third = packed[2 * block :]
    ref[index, : 2 * block + half] = packed
    ref[index, 2 * block + half : 3 * block] = pltpu.roll(third, 2 * block, 1)
    ref[index, 3 * block :] = pltpu.roll(packed[block : 2 * block], 3 * block, 1)


def gram_kernel(n_terms, *refs):
    terms = refs[:n_terms]
    gram_ref, near_ref, far_ref, keep_ref, hold_ref = refs[n_terms:]
    total = terms[0][...]
    for term in terms[1:]:
        total = total + term[...]
    gram_ref[...] = pack(dot_full(total, total, ((1,), (1,))))
    hold_ref[...] = total.T
    quarter = keep_ref.shape[0]

    def rows_of(m):
        at = pl.multiple_of(jnp.bitwise_xor(lax.axis_index("grp"), m) * quarter, quarter)
        return hold_ref[pl.ds(at, quarter), :]

    near_ref[:quarter] = rows_of(1)
    near_ref[quarter:] = rows_of(3)
    far_ref[...] = rows_of(2)
    keep_ref[...] = rows_of(0)


def gram_of(terms, n_grp):
    p, rows = terms[0].shape
    quarter = rows // n_grp
    return pl.pallas_call(
        functools.partial(gram_kernel, len(terms)),
        out_shape=tuple(
            jax.ShapeDtypeStruct((height, p), f32)
            for height in (p // 8 * 5, 2 * quarter, quarter, quarter)
        ),
        in_specs=[VM] * len(terms),
        out_specs=(VM, VM, VM, VM),
        scratch_shapes=[pltpu.VMEM((rows, p), f32)],
        compiler_params=pltpu.CompilerParams(vmem_limit_bytes=8 << 20),
        name="gram",
    )(*terms)


def split3(x):
    high = x.astype(bf16)
    rest = x - high.astype(f32)
    mid = rest.astype(bf16)
    return high, mid, (rest - mid.astype(f32)).astype(bf16)


def factor(m_ref, panel, group):
    count, p, _ = m_ref.shape
    lane = lax.broadcasted_iota(jnp.int32, (1, 1, p), 2)
    sub8 = lax.broadcasted_iota(jnp.int32, (1, 8, p), 1)
    n_tiles = panel // 8
    for base in range(0, p, panel):
        after = base + panel
        x = [m_ref[:, base + 8 * i : base + 8 * i + 8, :] for i in range(n_tiles)]
        for t0 in range(0, panel, group):
            i0 = t0 // 8
            tiles = range(i0, n_tiles)
            columns = []
            for s in range(t0, t0 + group):
                k = base + s
                columns.append([jnp.broadcast_to(x[i][:, :, k : k + 1], x[i].shape) for i in tiles])
            for t in range(group):
                ts = (t0 + t) % 8
                hit = lane == base + t0 + t
                scale = lax.rsqrt(columns[t][0][:, ts : ts + 1, :])
                parts = [column * scale for column in columns[t]]
                for s in range(t + 1, group):
                    ss = (t0 + s) % 8
                    weight = parts[0][:, ss : ss + 1, :]
                    columns[s] = [c - part * weight for c, part in zip(columns[s], parts)]
                row = jnp.where(hit, 1.0, x[i0][:, ts : ts + 1, :]) * scale
                for i in tiles:
                    new = jnp.where(hit, 0.0, x[i]) - parts[i - i0] * row
                    if i == i0:
                        new = jnp.where(sub8 < ts, x[i], jnp.where(sub8 == ts, row, new))
                    x[i] = new
        for i in range(n_tiles):
            m_ref[:, base + 8 * i : base + 8 * i + 8, :] = x[i]
        if after < p:
            for b in range(count):
                block = m_ref[b, base:after, :]
                si = lax.broadcasted_iota(jnp.int32, block.shape, 0)
                li = lax.broadcasted_iota(jnp.int32, block.shape, 1)
                right = jnp.where((li < after) & (li - base > si), 0.0, block)
                high, mid, low = split3(block)
                r_high, r_mid, r_low = split3(right)
                zero = jnp.zeros_like(r_low)
                lhs = jnp.concatenate([high, mid, low, high], axis=0).T[after:, :]
                first = jnp.concatenate([r_high, r_high, r_high, r_low], axis=0)
                second = jnp.concatenate([r_mid, r_mid, zero, zero], axis=0)
                rhs = jnp.concatenate([first, second], axis=1)
                both = jnp.dot(lhs, rhs, preferred_element_type=f32)
                change = both[:, :p] + both[:, p:]
                old = m_ref[b, after:, :]
                lj = lax.broadcasted_iota(jnp.int32, old.shape, 1)
                old = jnp.where((lj >= base) & (lj < after), 0.0, old)
                m_ref[b, after:, :] = old - change


def applied(x, solve):
    p = x.shape[1]
    high, low = split(x)
    dims = (((1,), (1,)), ((), ()))
    both = lax.dot_general(high, solve, dims, preferred_element_type=f32)
    both = both + lax.dot_general(low, solve, dims, preferred_element_type=f32)
    return both[:, :p] + both[:, p:]


def tree_kernel(panel, group, n_leaf, n_levels, *refs):
    grams = refs[:n_leaf]
    lefts = refs[n_leaf : n_leaf + n_levels]
    rights = refs[n_leaf + n_levels : n_leaf + 2 * n_levels]
    solve_ref, tr_ref, m_ref, pick_ref = refs[n_leaf + 2 * n_levels :]
    p = m_ref.shape[1]
    own = lax.axis_index("grp")
    device = lax.axis_index("dev")
    for m in range(n_leaf):
        unpack_to(m_ref, jnp.bitwise_xor(own, m), grams[m][...])
    m_ref[4] = m_ref[0] + m_ref[1]
    m_ref[5] = m_ref[2] + m_ref[3]
    m_ref[6] = m_ref[4] + m_ref[5]
    pick_ref[0] = grams[0][...]
    pick_ref[1] = grams[1][...]
    for level in range(n_levels):

        @pl.when(device % 2 ** (level + 1) == 2**level - 1)
        def _(level=level):
            pick_ref[0] = lefts[level][...]
            pick_ref[1] = rights[level][...]

    unpack_to(m_ref, 7, pick_ref[0])
    unpack_to(m_ref, 8, pick_ref[1])
    m_ref[9] = m_ref[7] + m_ref[8]
    factor(m_ref, panel, group)
    ri = lax.broadcasted_iota(jnp.int32, (p, p), 0)
    ci = lax.broadcasted_iota(jnp.int32, (p, p), 1)

    def inverse(b):
        return jnp.concatenate(split(jnp.where(ci <= ri, m_ref[b], 0.0)), axis=0)

    def upper(b):
        whole = m_ref[b]
        return jnp.where(ci > ri, whole, jnp.where(ci == ri, 1.0 / whole, 0.0))

    for leaf in range(n_leaf):
        solve_ref[leaf] = inverse(leaf)
    keep = device != lax.axis_size("dev") - 1
    for q, (a, b, node) in enumerate(((0, 1, 4), (2, 3, 5), (4, 5, 6), (7, 8, 9))):
        made = applied(jnp.concatenate([upper(a), upper(b)], axis=0), inverse(node))
        tr_ref[q] = jnp.where(keep, made, 0.0) if q == 3 else made


def tree(grams, lefts, rights, group=4):
    p = grams[0].shape[1]
    panel = p // 4
    n_leaf = len(grams)
    arrays = [*grams, *lefts, *rights]
    return pl.pallas_call(
        functools.partial(tree_kernel, panel, group, n_leaf, len(lefts)),
        out_shape=(
            jax.ShapeDtypeStruct((n_leaf, 2 * p, p), bf16),
            jax.ShapeDtypeStruct((4, 2 * p, p), f32),
        ),
        in_specs=[VM] * len(arrays),
        out_specs=(VM, VM),
        scratch_shapes=[pltpu.VMEM((10, p, p), f32), pltpu.VMEM((2, *grams[0].shape), f32)],
        compiler_params=pltpu.CompilerParams(vmem_limit_bytes=16 << 20),
        cost_estimate=pl.CostEstimate(flops=0, bytes_accessed=24 << 20, transcendentals=0),
        name="tree",
    )(*arrays)


def basis_kernel(solve_ref, own_ref, near_ref, far_ref, basis_ref):
    own = lax.axis_index("grp")
    quarter = own_ref.shape[0]
    rows = (own_ref[...], near_ref[:quarter], far_ref[:quarter], far_ref[quarter:])
    for m, value in enumerate(rows):
        leaf = jnp.bitwise_xor(own, m)
        basis_ref[leaf] = applied(value, solve_ref[leaf])


def basis(solves, own, near, far):
    n_leaf = solves.shape[0]
    quarter, p = own.shape
    return pl.pallas_call(
        basis_kernel,
        out_shape=jax.ShapeDtypeStruct((n_leaf, quarter, p), f32),
        in_specs=[VM] * 4,
        out_specs=VM,
        compiler_params=pltpu.CompilerParams(vmem_limit_bytes=8 << 20),
        name="basis",
    )(solves, own, near, far)


def gathered(omega, dev_count):
    n_local = omega.shape[0]
    half = n_local // 2
    masks = [2**bit for bit in range(1, dev_count.bit_length() - 1)]
    waves = {}
    for order, first in ((masks, 0), (masks[::-1], half)):
        held = [(0, 0, omega[first : first + half])]
        for place, mask in enumerate(order):
            new = [
                (max(level, place) + (seen > 0), seen ^ mask, value) for level, seen, value in held
            ]
            for at, (level, seen, value) in enumerate(new):
                new[at] = (level, seen, swapped(value, "dev", mask))
            for level, seen, value in new:
                waves.setdefault(level, []).append((seen, first, value))
            held = held + new
    other = swapped(omega, "dev", 1)
    order = [mask * n_local + q for mask in (0, 1) for q in range(n_local)]
    groups = [[omega[:half], omega[half:], other]]
    for level in sorted(waves):
        wave = waves[level]
        for flip in (0, 1):
            for seen, first, value in wave:
                order.extend((seen ^ flip) * n_local + first + q for q in range(half))

        values = [value for _, _, value in wave]
        others = [swapped(value, "dev", 1) for value in values]
        if level == 0:
            groups.append(values + others)
        else:
            groups.extend([values, others])
    return groups, order


def on_device(omega, u_factor, v_factor, columns, ranks):
    n_local, n_blocks = u_factor.shape[1:3]
    leaf_rows, width = u_factor.shape[3:]
    dev_count = lax.axis_size("dev")
    grp_count = lax.axis_size("grp")
    assert n_local == grp_count == 4
    clusters = n_local * dev_count
    most = -(-11 * n_local * n_blocks // (10 * clusters))
    v = jnp.swapaxes(v_factor[0], 2, 3).reshape(n_local * n_blocks, width, leaf_rows)
    u = jnp.swapaxes(u_factor[0], 2, 3).reshape(n_local * n_blocks, width, leaf_rows)
    groups, order = gathered(omega[0], dev_count)
    depth = -(-most // 8) * 8
    unit = 2 * width
    columns = jnp.swapaxes(columns[0], 1, 2)
    slots, v = slot_table(tuple(order), columns, ranks[0], v, depth, unit, n_local)
    coeff = None
    start = 0
    for index, pieces in enumerate(groups):
        ahead = u if index == len(groups) - 4 else None
        coeff = coefficients(slots, v, pieces, start, most, unit, coeff, ahead)
        start += sum(piece.shape[0] for piece in pieces)
    made = {}
    for m in (3, 2, 1, 0):
        made[m] = sketch(coeff, u, m, n_blocks)
    across = swapped(made[3], "grp", 1)
    across = swapped(made[2] + across, "grp", 2)
    beside = swapped(made[1], "grp", 1)
    gram, rows_near, rows_far, rows_own = gram_of([made[0], beside, across], grp_count)
    near_in = swapped(gram, "grp", 1)
    far_in = swapped(gram, "grp", 2)
    pass_in = swapped(near_in, "grp", 2)
    rows_near = swapped(rows_near, "grp", 1)
    grams = [gram, near_in, far_in, pass_in]
    current = (gram + near_in) + (far_in + pass_in)
    lefts, rights = [], []
    masks = [2**bit for bit in range(dev_count.bit_length() - 1)]
    steps = [masks[:1]] + [masks[at : at + 2] for at in range(1, len(masks), 2)]
    for step in steps:
        first = swapped(current, "dev", step[0])
        wider = [swapped(current, "dev", extra ^ step[1]) for extra in (0, step[0])] if step[1:] else []
        lefts.append(current)
        rights.append(first)
        current = current + first
        if wider:
            lefts.append(current)
            rights.append(wider[0] + wider[1])
            current = current + rights[-1]
    quarter = rows_own.shape[0]
    rows_far = swapped(jnp.concatenate([rows_far, rows_near[quarter:]]), "grp", 2)
    solves, transfer = tree(grams, lefts, rights)
    return basis(solves, rows_own, rows_near, rows_far), transfer


def solution(mesh):
    placed = (
        P("grp", "dev", None, None),
        P("grp", "dev", None, None, None),
        P("grp", "dev", None, None, None),
        P("grp", "dev", None, None),
        P("grp", "dev", None),
    )
    return jax.shard_map(
        on_device,
        mesh=mesh,
        in_specs=placed,
        out_specs=(P("dev", "grp", None), P("dev", None, None)),
        check_vma=False,
    )
```

```python
import functools

import jax
import jax.numpy as jnp
from jax import lax
from jax.experimental import pallas as pl
from jax.experimental.pallas import tpu as pltpu
from jax.sharding import PartitionSpec as P


f32 = jnp.float32
bf16 = jnp.bfloat16
VM = pl.BlockSpec(memory_space=pltpu.VMEM)
SM = pl.BlockSpec(memory_space=pltpu.SMEM)


def swapped(value, axis, mask):
    pairs = [(source, source ^ mask) for source in range(lax.axis_size(axis))]
    return lax.ppermute(value, axis, pairs)


def split(x):
    high = x.astype(bf16)
    low = (x - high.astype(f32)).astype(bf16)
    return high, low


def dot_full(x, y, dims):
    return lax.dot_general(
        x, y, (dims, ((), ())), precision=lax.Precision.HIGHEST, preferred_element_type=f32
    )


def in_hbm(x):
    return pltpu.with_memory_space_constraint(x, pltpu.HBM)


def table_kernel(order, unit, n_local, cols_ref, ranks_ref, v_ref, slot_ref, held_ref, sem):
    copy = pltpu.make_async_copy(v_ref, held_ref, sem)
    copy.start()
    n_leaf, _, n_blocks = cols_ref.shape
    depth, clusters = slot_ref.shape
    position = lax.broadcasted_iota(jnp.int32, (clusters, 1), 0)
    names = jnp.zeros((clusters, 1), jnp.int32)
    for at, cluster in enumerate(order):
        names = jnp.where(position == at, cluster, names)
    names = jnp.bitwise_xor(names, lax.axis_index("dev") * n_local)
    ones = jnp.ones((n_blocks, n_blocks), bf16)
    si = lax.broadcasted_iota(jnp.int32, (n_blocks, n_blocks), 0)
    li = lax.broadcasted_iota(jnp.int32, (n_blocks, n_blocks), 1)
    before = jnp.where(si < li, 1.0, 0.0).astype(bf16)
    number = lax.broadcasted_iota(jnp.int32, (depth, n_blocks), 1).astype(f32)
    level = lax.broadcasted_iota(jnp.int32, (depth, n_blocks), 0).astype(f32)
    offset = jnp.zeros((clusters, n_blocks), f32)
    index = jnp.zeros((depth, clusters), f32)
    rank = jnp.zeros((depth, clusters), f32)
    used = jnp.zeros((depth, clusters), f32)
    for c in range(n_leaf):
        named = jnp.where(cols_ref[c] == names, 1.0, 0.0)
        named_low = named.astype(bf16)

        def listed(x, named_low=named_low):
            return lax.dot_general(
                x.astype(bf16), named_low, (((1,), (1,)), ((), ())), preferred_element_type=f32
            )

        ahead = offset + jnp.dot(named_low, before, preferred_element_type=f32)
        place = jnp.sum(named * ahead, axis=0, keepdims=True)
        mark = jnp.where(place == level, 1.0, 0.0)
        here = listed(mark)
        index = index + listed(mark * number) + here * float(c * n_blocks)
        rank = rank + listed(mark * ranks_ref[c : c + 1, :].astype(f32))
        used = used + here
        offset = offset + jnp.dot(named_low, ones, preferred_element_type=f32)
    index = jnp.where(used > 0.5, index, float(n_leaf * n_blocks))
    slot_ref[...] = index.astype(jnp.int32) * unit + rank.astype(jnp.int32)
    copy.wait()


def slot_table(order, cols, ranks, v, depth, unit, n_local):
    return pl.pallas_call(
        functools.partial(table_kernel, order, unit, n_local),
        out_shape=(
            jax.ShapeDtypeStruct((depth, len(order)), jnp.int32),
            jax.ShapeDtypeStruct(v.shape, f32),
        ),
        in_specs=[VM, VM, pl.BlockSpec(memory_space=pltpu.HBM)],
        out_specs=(VM, VM),
        scratch_shapes=[pltpu.SemaphoreType.DMA],
        compiler_params=pltpu.CompilerParams(vmem_limit_bytes=4 << 20),
        cost_estimate=pl.CostEstimate(flops=0, bytes_accessed=24 << 20, transcendentals=0),
        name="slots",
    )(cols, ranks, in_hbm(v))


def coeff_kernel(most, start, unit, n_pieces, *refs):
    slot_ref, v_ref = refs[:2]
    pieces = refs[2 : 2 + n_pieces]
    c_ref, w_ref = refs[-2:]
    p = pieces[0].shape[2]
    n_all, k, _ = v_ref.shape
    at = 0
    for piece in pieces:
        for q in range(piece.shape[0]):
            high, low = split(piece[q])
            w_ref[at, :, :p] = high
            w_ref[at, :, p:] = low
            at += 1
    sub = lax.broadcasted_iota(jnp.int32, (k, p), 0)

    def body(j, _):
        highs, lows, ids, kept = [], [], [], []
        for n in range(most):
            entry = slot_ref[n, start + j]
            b = entry // unit
            ids.append(b)
            kept.append(sub < entry % unit)
            high, low = split(v_ref[jnp.minimum(b, n_all - 1)])
            highs.append(high)
            lows.append(low)
        w = w_ref[j]
        both = jnp.dot(jnp.concatenate(highs + lows, 0), w, preferred_element_type=f32)
        both = both[: most * k] + both[most * k :]
        total = both[:, :p] + both[:, p:]
        for n in range(most):
            c_ref[ids[n]] = jnp.where(kept[n], total[n * k : (n + 1) * k], 0.0)
        return 0

    lax.fori_loop(0, at, body, 0, unroll=4)


def coefficients(slots, v, pieces, start, most, unit, before, ahead):
    n_all, k, rows = v.shape
    p = pieces[0].shape[2]
    held = sum(piece.shape[0] for piece in pieces)
    args = [slots, v, *pieces] + [value for value in (ahead, before) if value is not None]
    return pl.pallas_call(
        functools.partial(coeff_kernel, most, start, unit, len(pieces)),
        out_shape=jax.ShapeDtypeStruct((n_all + 1, k, p), f32),
        in_specs=[SM] + [VM] * (len(args) - 1),
        out_specs=VM,
        scratch_shapes=[pltpu.VMEM((held, rows, 2 * p), bf16)],
        input_output_aliases={} if before is None else {len(args) - 1: 0},
        compiler_params=pltpu.CompilerParams(vmem_limit_bytes=12 << 20),
        cost_estimate=pl.CostEstimate(
            flops=0, bytes_accessed=held * 192 << 10, transcendentals=0
        ),
        name="coeff",
    )(*args)


def sketch_kernel(m, n_blocks, c_ref, u_ref, o_ref):
    p, rows = o_ref.shape
    k = u_ref.shape[1]
    step = rows // k
    leaf = jnp.bitwise_xor(lax.axis_index("grp"), m)
    both = jnp.zeros((2 * p, rows), f32)
    total = jnp.zeros((p, rows), f32)
    for q in range(n_blocks // step):
        at = pl.ds(leaf * n_blocks + q * step, step)
        high, low = split(c_ref[at].reshape(rows, p).T)
        u_high, u_low = split(u_ref[at].reshape(rows, rows))
        pair = jnp.concatenate([high, low], axis=0)
        both = both + jnp.dot(pair, u_high, preferred_element_type=f32)
        total = total + jnp.dot(high, u_low, preferred_element_type=f32)
    o_ref[...] = total + both[:p] + both[p:]


def sketch(coeff, u, m, n_blocks):
    k, rows = u.shape[1:]
    p = coeff.shape[2]
    return pl.pallas_call(
        functools.partial(sketch_kernel, m, n_blocks),
        out_shape=jax.ShapeDtypeStruct((p, rows), f32),
        in_specs=[VM, VM],
        out_specs=VM,
        compiler_params=pltpu.CompilerParams(vmem_limit_bytes=8 << 20),
        cost_estimate=pl.CostEstimate(
            flops=n_blocks * k * rows * p * 6, bytes_accessed=1 << 20, transcendentals=0
        ),
        name="sketch",
    )(coeff, u)


def pack(gram):
    p = gram.shape[0]
    block = p // 4
    half = block // 2
    lane = lax.broadcasted_iota(jnp.int32, (block, p), 1)
    second = jnp.where(lane < block, pltpu.roll(gram[3 * block :], block, 1), gram[block : 2 * block])
    third = gram[2 * block : 3 * block]
    third = jnp.where(lane[:half] < 2 * block, pltpu.roll(third[half:], 2 * block, 1), third[:half])
    return jnp.concatenate([gram[:block], second, third], axis=0)


def unpack_to(ref, index, packed):
    p = packed.shape[1]
    block = p // 4
    half = block // 2
    third = packed[2 * block :]
    ref[index, : 2 * block + half] = packed
    ref[index, 2 * block + half : 3 * block] = pltpu.roll(third, 2 * block, 1)
    ref[index, 3 * block :] = pltpu.roll(packed[block : 2 * block], 3 * block, 1)


def gram_kernel(n_terms, *refs):
    terms = refs[:n_terms]
    gram_ref, near_ref, far_ref, keep_ref, hold_ref = refs[n_terms:]
    total = terms[0][...]
    for term in terms[1:]:
        total = total + term[...]
    gram_ref[...] = pack(dot_full(total, total, ((1,), (1,))))
    hold_ref[...] = total.T
    quarter = keep_ref.shape[0]

    def rows_of(m):
        at = pl.multiple_of(jnp.bitwise_xor(lax.axis_index("grp"), m) * quarter, quarter)
        return hold_ref[pl.ds(at, quarter), :]

    near_ref[:quarter] = rows_of(1)
    near_ref[quarter:] = rows_of(3)
    far_ref[...] = rows_of(2)
    keep_ref[...] = rows_of(0)


def gram_of(terms, n_grp):
    p, rows = terms[0].shape
    quarter = rows // n_grp
    return pl.pallas_call(
        functools.partial(gram_kernel, len(terms)),
        out_shape=tuple(
            jax.ShapeDtypeStruct((height, p), f32)
            for height in (p // 8 * 5, 2 * quarter, quarter, quarter)
        ),
        in_specs=[VM] * len(terms),
        out_specs=(VM, VM, VM, VM),
        scratch_shapes=[pltpu.VMEM((rows, p), f32)],
        compiler_params=pltpu.CompilerParams(vmem_limit_bytes=8 << 20),
        name="gram",
    )(*terms)


def split3(x):
    high = x.astype(bf16)
    rest = x - high.astype(f32)
    mid = rest.astype(bf16)
    return high, mid, (rest - mid.astype(f32)).astype(bf16)


def factor(m_ref, panel, group):
    count, p, _ = m_ref.shape
    lane = lax.broadcasted_iota(jnp.int32, (1, 1, p), 2)
    sub8 = lax.broadcasted_iota(jnp.int32, (1, 8, p), 1)
    n_tiles = panel // 8
    for base in range(0, p, panel):
        after = base + panel
        x = [m_ref[:, base + 8 * i : base + 8 * i + 8, :] for i in range(n_tiles)]
        for t0 in range(0, panel, group):
            i0 = t0 // 8
            tiles = range(i0, n_tiles)
            columns = []
            for s in range(t0, t0 + group):
                k = base + s
                columns.append([jnp.broadcast_to(x[i][:, :, k : k + 1], x[i].shape) for i in tiles])
            for t in range(group):
                ts = (t0 + t) % 8
                hit = lane == base + t0 + t
                scale = lax.rsqrt(columns[t][0][:, ts : ts + 1, :])
                parts = [column * scale for column in columns[t]]
                for s in range(t + 1, group):
                    ss = (t0 + s) % 8
                    weight = parts[0][:, ss : ss + 1, :]
                    columns[s] = [c - part * weight for c, part in zip(columns[s], parts)]
                row = jnp.where(hit, 1.0, x[i0][:, ts : ts + 1, :]) * scale
                for i in tiles:
                    new = jnp.where(hit, 0.0, x[i]) - parts[i - i0] * row
                    if i == i0:
                        new = jnp.where(sub8 < ts, x[i], jnp.where(sub8 == ts, row, new))
                    x[i] = new
        for i in range(n_tiles):
            m_ref[:, base + 8 * i : base + 8 * i + 8, :] = x[i]
        if after < p:
            for b in range(count):
                block = m_ref[b, base:after, :]
                si = lax.broadcasted_iota(jnp.int32, block.shape, 0)
                li = lax.broadcasted_iota(jnp.int32, block.shape, 1)
                right = jnp.where((li < after) & (li - base > si), 0.0, block)
                high, mid, low = split3(block)
                r_high, r_mid, r_low = split3(right)
                zero = jnp.zeros_like(r_low)
                lhs = jnp.concatenate([high, mid, low, high], axis=0).T[after:, :]
                first = jnp.concatenate([r_high, r_high, r_high, r_low], axis=0)
                second = jnp.concatenate([r_mid, r_mid, zero, zero], axis=0)
                rhs = jnp.concatenate([first, second], axis=1)
                both = jnp.dot(lhs, rhs, preferred_element_type=f32)
                change = both[:, :p] + both[:, p:]
                old = m_ref[b, after:, :]
                lj = lax.broadcasted_iota(jnp.int32, old.shape, 1)
                old = jnp.where((lj >= base) & (lj < after), 0.0, old)
                m_ref[b, after:, :] = old - change


def applied(x, solve):
    p = x.shape[1]
    high, low = split(x)
    dims = (((1,), (1,)), ((), ()))
    both = jnp.concatenate([high, low], axis=0)
    both = lax.dot_general(both, solve, dims, preferred_element_type=f32)
    both = both[: x.shape[0]] + both[x.shape[0] :]
    return both[:, :p] + both[:, p:]


def tree_kernel(panel, group, n_leaf, n_levels, *refs):
    grams = refs[:n_leaf]
    lefts = refs[n_leaf : n_leaf + n_levels]
    rights = refs[n_leaf + n_levels : n_leaf + 2 * n_levels]
    solve_ref, tr_ref, m_ref, pick_ref = refs[n_leaf + 2 * n_levels :]
    p = m_ref.shape[1]
    own = lax.axis_index("grp")
    device = lax.axis_index("dev")
    for m in range(n_leaf):
        unpack_to(m_ref, jnp.bitwise_xor(own, m), grams[m][...])
    m_ref[4] = m_ref[0] + m_ref[1]
    m_ref[5] = m_ref[2] + m_ref[3]
    m_ref[6] = m_ref[4] + m_ref[5]
    pick_ref[0] = grams[0][...]
    pick_ref[1] = grams[1][...]
    for level in range(n_levels):

        @pl.when(device % 2 ** (level + 1) == 2**level - 1)
        def _(level=level):
            pick_ref[0] = lefts[level][...]
            pick_ref[1] = rights[level][...]

    unpack_to(m_ref, 7, pick_ref[0])
    unpack_to(m_ref, 8, pick_ref[1])
    m_ref[9] = m_ref[7] + m_ref[8]
    factor(m_ref, panel, group)
    ri = lax.broadcasted_iota(jnp.int32, (p, p), 0)
    ci = lax.broadcasted_iota(jnp.int32, (p, p), 1)

    def inverse(b):
        return jnp.concatenate(split(jnp.where(ci <= ri, m_ref[b], 0.0)), axis=0)

    def upper(b):
        whole = m_ref[b]
        return jnp.where(ci > ri, whole, jnp.where(ci == ri, 1.0 / whole, 0.0))

    for leaf in range(n_leaf):
        solve_ref[leaf] = inverse(leaf)
    keep = device != lax.axis_size("dev") - 1
    for q, (a, b, node) in enumerate(((0, 1, 4), (2, 3, 5), (4, 5, 6), (7, 8, 9))):
        made = applied(jnp.concatenate([upper(a), upper(b)], axis=0), inverse(node))
        tr_ref[q] = jnp.where(keep, made, 0.0) if q == 3 else made


def tree(grams, lefts, rights, group=4):
    p = grams[0].shape[1]
    panel = p // 4
    n_leaf = len(grams)
    arrays = [*grams, *lefts, *rights]
    return pl.pallas_call(
        functools.partial(tree_kernel, panel, group, n_leaf, len(lefts)),
        out_shape=(
            jax.ShapeDtypeStruct((n_leaf, 2 * p, p), bf16),
            jax.ShapeDtypeStruct((4, 2 * p, p), f32),
        ),
        in_specs=[VM] * len(arrays),
        out_specs=(VM, VM),
        scratch_shapes=[pltpu.VMEM((10, p, p), f32), pltpu.VMEM((2, *grams[0].shape), f32)],
        compiler_params=pltpu.CompilerParams(vmem_limit_bytes=16 << 20),
        cost_estimate=pl.CostEstimate(flops=0, bytes_accessed=24 << 20, transcendentals=0),
        name="tree",
    )(*arrays)


def basis_kernel(solve_ref, own_ref, near_ref, far_ref, basis_ref):
    own = lax.axis_index("grp")
    quarter = own_ref.shape[0]
    rows = (own_ref[...], near_ref[:quarter], far_ref[:quarter], far_ref[quarter:])
    for m, value in enumerate(rows):
        leaf = jnp.bitwise_xor(own, m)
        basis_ref[leaf] = applied(value, solve_ref[leaf])


def basis(solves, own, near, far):
    n_leaf = solves.shape[0]
    quarter, p = own.shape
    return pl.pallas_call(
        basis_kernel,
        out_shape=jax.ShapeDtypeStruct((n_leaf, quarter, p), f32),
        in_specs=[VM] * 4,
        out_specs=VM,
        compiler_params=pltpu.CompilerParams(vmem_limit_bytes=8 << 20),
        name="basis",
    )(solves, own, near, far)


def gathered(omega, dev_count):
    n_local = omega.shape[0]
    half = n_local // 2
    masks = [2**bit for bit in range(1, dev_count.bit_length() - 1)]
    waves = {}
    for order, first in ((masks, 0), (masks[::-1], half)):
        held = [(0, 0, omega[first : first + half])]
        for place, mask in enumerate(order):
            new = [
                (max(level, place) + (seen > 0), seen ^ mask, value) for level, seen, value in held
            ]
            for at, (level, seen, value) in enumerate(new):
                new[at] = (level, seen, swapped(value, "dev", mask))
            for level, seen, value in new:
                waves.setdefault(level, []).append((seen, first, value))
            held = held + new
    other = swapped(omega, "dev", 1)
    order = [mask * n_local + q for mask in (0, 1) for q in range(n_local)]
    groups = [[omega[:half], omega[half:], other]]
    for level in sorted(waves):
        wave = waves[level]
        for flip in (0, 1):
            for seen, first, value in wave:
                order.extend((seen ^ flip) * n_local + first + q for q in range(half))

        values = [value for _, _, value in wave]
        others = [swapped(value, "dev", 1) for value in values]
        if level == 0:
            groups.append(values + others)
        else:
            groups.extend([values, others])
    return groups, order


def on_device(omega, u_factor, v_factor, columns, ranks):
    n_local, n_blocks = u_factor.shape[1:3]
    leaf_rows, width = u_factor.shape[3:]
    dev_count = lax.axis_size("dev")
    grp_count = lax.axis_size("grp")
    assert n_local == grp_count == 4
    clusters = n_local * dev_count
    most = -(-11 * n_local * n_blocks // (10 * clusters))
    v = jnp.swapaxes(v_factor[0], 2, 3).reshape(n_local * n_blocks, width, leaf_rows)
    u = jnp.swapaxes(u_factor[0], 2, 3).reshape(n_local * n_blocks, width, leaf_rows)
    groups, order = gathered(omega[0], dev_count)
    depth = -(-most // 8) * 8
    unit = 2 * width
    columns = jnp.swapaxes(columns[0], 1, 2)
    slots, v = slot_table(tuple(order), columns, ranks[0], v, depth, unit, n_local)
    coeff = None
    start = 0
    for index, pieces in enumerate(groups):
        ahead = u if index == len(groups) - 4 else None
        coeff = coefficients(slots, v, pieces, start, most, unit, coeff, ahead)
        start += sum(piece.shape[0] for piece in pieces)
    made = {}
    for m in (3, 2, 1, 0):
        made[m] = sketch(coeff, u, m, n_blocks)
    across = swapped(made[3], "grp", 1)
    across = swapped(made[2] + across, "grp", 2)
    beside = swapped(made[1], "grp", 1)
    gram, rows_near, rows_far, rows_own = gram_of([made[0], beside, across], grp_count)
    near_in = swapped(gram, "grp", 1)
    far_in = swapped(gram, "grp", 2)
    pass_in = swapped(near_in, "grp", 2)
    rows_near = swapped(rows_near, "grp", 1)
    grams = [gram, near_in, far_in, pass_in]
    current = (gram + near_in) + (far_in + pass_in)
    lefts, rights = [], []
    masks = [2**bit for bit in range(dev_count.bit_length() - 1)]
    steps = [masks[:1]] + [masks[at : at + 2] for at in range(1, len(masks), 2)]
    for step in steps:
        first = swapped(current, "dev", step[0])
        wider = [swapped(current, "dev", extra ^ step[1]) for extra in (0, step[0])] if step[1:] else []
        lefts.append(current)
        rights.append(first)
        current = current + first
        if wider:
            lefts.append(current)
            rights.append(wider[0] + wider[1])
            current = current + rights[-1]
    quarter = rows_own.shape[0]
    rows_far = swapped(jnp.concatenate([rows_far, rows_near[quarter:]]), "grp", 2)
    solves, transfer = tree(grams, lefts, rights)
    return basis(solves, rows_own, rows_near, rows_far), transfer


def solution(mesh):
    placed = (
        P("grp", "dev", None, None),
        P("grp", "dev", None, None, None),
        P("grp", "dev", None, None, None),
        P("grp", "dev", None, None),
        P("grp", "dev", None),
    )
    return jax.shard_map(
        on_device,
        mesh=mesh,
        in_specs=placed,
        out_specs=(P("dev", "grp", None), P("dev", None, None)),
        check_vma=False,
    )
```

```python
import functools

import jax
import jax.numpy as jnp
from jax import lax
from jax.experimental import pallas as pl
from jax.experimental.pallas import tpu as pltpu
from jax.sharding import PartitionSpec as P


f32 = jnp.float32
bf16 = jnp.bfloat16
VM = pl.BlockSpec(memory_space=pltpu.VMEM)
SM = pl.BlockSpec(memory_space=pltpu.SMEM)


def swapped(value, axis, mask):
    pairs = [(source, source ^ mask) for source in range(lax.axis_size(axis))]
    return lax.ppermute(value, axis, pairs)


def split(x):
    high = x.astype(bf16)
    low = (x - high.astype(f32)).astype(bf16)
    return high, low


def dot_full(x, y, dims):
    return lax.dot_general(
        x, y, (dims, ((), ())), precision=lax.Precision.HIGHEST, preferred_element_type=f32
    )


def in_hbm(x):
    return pltpu.with_memory_space_constraint(x, pltpu.HBM)


def table_kernel(order, unit, n_local, cols_ref, ranks_ref, v_ref, slot_ref, held_ref, sem):
    copy = pltpu.make_async_copy(v_ref, held_ref, sem)
    copy.start()
    n_leaf, _, n_blocks = cols_ref.shape
    depth, clusters = slot_ref.shape
    position = lax.broadcasted_iota(jnp.int32, (clusters, 1), 0)
    names = jnp.zeros((clusters, 1), jnp.int32)
    for at, cluster in enumerate(order):
        names = jnp.where(position == at, cluster, names)
    names = jnp.bitwise_xor(names, lax.axis_index("dev") * n_local)
    ones = jnp.ones((n_blocks, n_blocks), bf16)
    si = lax.broadcasted_iota(jnp.int32, (n_blocks, n_blocks), 0)
    li = lax.broadcasted_iota(jnp.int32, (n_blocks, n_blocks), 1)
    before = jnp.where(si < li, 1.0, 0.0).astype(bf16)
    number = lax.broadcasted_iota(jnp.int32, (depth, n_blocks), 1).astype(f32)
    level = lax.broadcasted_iota(jnp.int32, (depth, n_blocks), 0).astype(f32)
    offset = jnp.zeros((clusters, n_blocks), f32)
    index = jnp.zeros((depth, clusters), f32)
    rank = jnp.zeros((depth, clusters), f32)
    used = jnp.zeros((depth, clusters), f32)
    for c in range(n_leaf):
        named = jnp.where(cols_ref[c] == names, 1.0, 0.0)
        named_low = named.astype(bf16)

        def listed(x, named_low=named_low):
            return lax.dot_general(
                x.astype(bf16), named_low, (((1,), (1,)), ((), ())), preferred_element_type=f32
            )

        ahead = offset + jnp.dot(named_low, before, preferred_element_type=f32)
        place = jnp.sum(named * ahead, axis=0, keepdims=True)
        mark = jnp.where(place == level, 1.0, 0.0)
        here = listed(mark)
        index = index + listed(mark * number) + here * float(c * n_blocks)
        rank = rank + listed(mark * ranks_ref[c : c + 1, :].astype(f32))
        used = used + here
        offset = offset + jnp.dot(named_low, ones, preferred_element_type=f32)
    index = jnp.where(used > 0.5, index, float(n_leaf * n_blocks))
    slot_ref[...] = index.astype(jnp.int32) * unit + rank.astype(jnp.int32)
    copy.wait()


def slot_table(order, cols, ranks, v, depth, unit, n_local):
    return pl.pallas_call(
        functools.partial(table_kernel, order, unit, n_local),
        out_shape=(
            jax.ShapeDtypeStruct((depth, len(order)), jnp.int32),
            jax.ShapeDtypeStruct(v.shape, f32),
        ),
        in_specs=[VM, VM, pl.BlockSpec(memory_space=pltpu.HBM)],
        out_specs=(VM, VM),
        scratch_shapes=[pltpu.SemaphoreType.DMA],
        compiler_params=pltpu.CompilerParams(vmem_limit_bytes=4 << 20),
        cost_estimate=pl.CostEstimate(flops=0, bytes_accessed=24 << 20, transcendentals=0),
        name="slots",
    )(cols, ranks, in_hbm(v))


def coeff_kernel(most, start, unit, n_pieces, *refs):
    slot_ref, v_ref = refs[:2]
    pieces = refs[2 : 2 + n_pieces]
    c_ref, w_ref = refs[-2:]
    p = pieces[0].shape[2]
    n_all, k, _ = v_ref.shape
    at = 0
    for piece in pieces:
        for q in range(piece.shape[0]):
            high, low = split(piece[q])
            w_ref[at, :, :p] = high
            w_ref[at, :, p:] = low
            at += 1
    sub = lax.broadcasted_iota(jnp.int32, (k, p), 0)

    def body(j, _):
        highs, lows, ids, kept = [], [], [], []
        for n in range(most):
            entry = slot_ref[n, start + j]
            b = entry // unit
            ids.append(b)
            kept.append(sub < entry % unit)
            high, low = split(v_ref[jnp.minimum(b, n_all - 1)])
            highs.append(high)
            lows.append(low)
        w = w_ref[j]
        both = jnp.dot(jnp.concatenate(highs, 0), w, preferred_element_type=f32)
        both = both + jnp.dot(jnp.concatenate(lows, 0), w, preferred_element_type=f32)
        total = both[:, :p] + both[:, p:]
        for n in range(most):
            c_ref[ids[n]] = jnp.where(kept[n], total[n * k : (n + 1) * k], 0.0)
        return 0

    lax.fori_loop(0, at, body, 0, unroll=8)


def coefficients(slots, v, pieces, start, most, unit, before, ahead):
    n_all, k, rows = v.shape
    p = pieces[0].shape[2]
    held = sum(piece.shape[0] for piece in pieces)
    args = [slots, v, *pieces] + [value for value in (ahead, before) if value is not None]
    return pl.pallas_call(
        functools.partial(coeff_kernel, most, start, unit, len(pieces)),
        out_shape=jax.ShapeDtypeStruct((n_all + 1, k, p), f32),
        in_specs=[SM] + [VM] * (len(args) - 1),
        out_specs=VM,
        scratch_shapes=[pltpu.VMEM((held, rows, 2 * p), bf16)],
        input_output_aliases={} if before is None else {len(args) - 1: 0},
        compiler_params=pltpu.CompilerParams(vmem_limit_bytes=12 << 20),
        cost_estimate=pl.CostEstimate(
            flops=0, bytes_accessed=held * 192 << 10, transcendentals=0
        ),
        name="coeff",
    )(*args)


def sketch_kernel(m, n_blocks, c_ref, u_ref, o_ref):
    p, rows = o_ref.shape
    k = u_ref.shape[1]
    step = rows // k
    leaf = jnp.bitwise_xor(lax.axis_index("grp"), m)
    both = jnp.zeros((2 * p, rows), f32)
    total = jnp.zeros((p, rows), f32)
    for q in range(n_blocks // step):
        at = pl.ds(leaf * n_blocks + q * step, step)
        high, low = split(c_ref[at].reshape(rows, p).T)
        u_high, u_low = split(u_ref[at].reshape(rows, rows))
        pair = jnp.concatenate([high, low], axis=0)
        both = both + jnp.dot(pair, u_high, preferred_element_type=f32)
        total = total + jnp.dot(high, u_low, preferred_element_type=f32)
    o_ref[...] = total + both[:p] + both[p:]


def sketch(coeff, u, m, n_blocks):
    k, rows = u.shape[1:]
    p = coeff.shape[2]
    return pl.pallas_call(
        functools.partial(sketch_kernel, m, n_blocks),
        out_shape=jax.ShapeDtypeStruct((p, rows), f32),
        in_specs=[VM, VM],
        out_specs=VM,
        compiler_params=pltpu.CompilerParams(vmem_limit_bytes=8 << 20),
        cost_estimate=pl.CostEstimate(
            flops=n_blocks * k * rows * p * 6, bytes_accessed=1 << 20, transcendentals=0
        ),
        name="sketch",
    )(coeff, u)


def pack(gram):
    p = gram.shape[0]
    block = p // 4
    half = block // 2
    lane = lax.broadcasted_iota(jnp.int32, (block, p), 1)
    second = jnp.where(lane < block, pltpu.roll(gram[3 * block :], block, 1), gram[block : 2 * block])
    third = gram[2 * block : 3 * block]
    third = jnp.where(lane[:half] < 2 * block, pltpu.roll(third[half:], 2 * block, 1), third[:half])
    return jnp.concatenate([gram[:block], second, third], axis=0)


def unpack_to(ref, index, packed):
    p = packed.shape[1]
    block = p // 4
    half = block // 2
    third = packed[2 * block :]
    ref[index, : 2 * block + half] = packed
    ref[index, 2 * block + half : 3 * block] = pltpu.roll(third, 2 * block, 1)
    ref[index, 3 * block :] = pltpu.roll(packed[block : 2 * block], 3 * block, 1)


def gram_kernel(n_terms, *refs):
    terms = refs[:n_terms]
    gram_ref, near_ref, far_ref, keep_ref, hold_ref = refs[n_terms:]
    total = terms[0][...]
    for term in terms[1:]:
        total = total + term[...]
    gram_ref[...] = pack(dot_full(total, total, ((1,), (1,))))
    hold_ref[...] = total.T
    quarter = keep_ref.shape[0]

    def rows_of(m):
        at = pl.multiple_of(jnp.bitwise_xor(lax.axis_index("grp"), m) * quarter, quarter)
        return hold_ref[pl.ds(at, quarter), :]

    near_ref[:quarter] = rows_of(1)
    near_ref[quarter:] = rows_of(3)
    far_ref[...] = rows_of(2)
    keep_ref[...] = rows_of(0)


def gram_of(terms, n_grp):
    p, rows = terms[0].shape
    quarter = rows // n_grp
    return pl.pallas_call(
        functools.partial(gram_kernel, len(terms)),
        out_shape=tuple(
            jax.ShapeDtypeStruct((height, p), f32)
            for height in (p // 8 * 5, 2 * quarter, quarter, quarter)
        ),
        in_specs=[VM] * len(terms),
        out_specs=(VM, VM, VM, VM),
        scratch_shapes=[pltpu.VMEM((rows, p), f32)],
        compiler_params=pltpu.CompilerParams(vmem_limit_bytes=8 << 20),
        name="gram",
    )(*terms)


def split3(x):
    high = x.astype(bf16)
    rest = x - high.astype(f32)
    mid = rest.astype(bf16)
    return high, mid, (rest - mid.astype(f32)).astype(bf16)


def factor(m_ref, panel, group):
    count, p, _ = m_ref.shape
    lane = lax.broadcasted_iota(jnp.int32, (1, 1, p), 2)
    sub8 = lax.broadcasted_iota(jnp.int32, (1, 8, p), 1)
    n_tiles = panel // 8
    for base in range(0, p, panel):
        after = base + panel
        x = [m_ref[:, base + 8 * i : base + 8 * i + 8, :] for i in range(n_tiles)]
        for t0 in range(0, panel, group):
            i0 = t0 // 8
            tiles = range(i0, n_tiles)
            columns = []
            for s in range(t0, t0 + group):
                k = base + s
                columns.append([jnp.broadcast_to(x[i][:, :, k : k + 1], x[i].shape) for i in tiles])
            for t in range(group):
                ts = (t0 + t) % 8
                hit = lane == base + t0 + t
                scale = lax.rsqrt(columns[t][0][:, ts : ts + 1, :])
                parts = [column * scale for column in columns[t]]
                for s in range(t + 1, group):
                    ss = (t0 + s) % 8
                    weight = parts[0][:, ss : ss + 1, :]
                    columns[s] = [c - part * weight for c, part in zip(columns[s], parts)]
                row = jnp.where(hit, 1.0, x[i0][:, ts : ts + 1, :]) * scale
                for i in tiles:
                    new = jnp.where(hit, 0.0, x[i]) - parts[i - i0] * row
                    if i == i0:
                        new = jnp.where(sub8 < ts, x[i], jnp.where(sub8 == ts, row, new))
                    x[i] = new
        for i in range(n_tiles):
            m_ref[:, base + 8 * i : base + 8 * i + 8, :] = x[i]
        if after < p:
            for b in range(count):
                block = m_ref[b, base:after, :]
                si = lax.broadcasted_iota(jnp.int32, block.shape, 0)
                li = lax.broadcasted_iota(jnp.int32, block.shape, 1)
                right = jnp.where((li < after) & (li - base > si), 0.0, block)
                high, mid, low = split3(block)
                r_high, r_mid, r_low = split3(right)
                zero = jnp.zeros_like(r_low)
                lhs = jnp.concatenate([high, mid, low, high], axis=0).T[after:, :]
                first = jnp.concatenate([r_high, r_high, r_high, r_low], axis=0)
                second = jnp.concatenate([r_mid, r_mid, zero, zero], axis=0)
                rhs = jnp.concatenate([first, second], axis=1)
                both = jnp.dot(lhs, rhs, preferred_element_type=f32)
                change = both[:, :p] + both[:, p:]
                old = m_ref[b, after:, :]
                lj = lax.broadcasted_iota(jnp.int32, old.shape, 1)
                old = jnp.where((lj >= base) & (lj < after), 0.0, old)
                m_ref[b, after:, :] = old - change


def applied(x, solve):
    p = x.shape[1]
    high, low = split(x)
    dims = (((1,), (1,)), ((), ()))
    both = lax.dot_general(high, solve, dims, preferred_element_type=f32)
    both = both + lax.dot_general(low, solve, dims, preferred_element_type=f32)
    return both[:, :p] + both[:, p:]


def tree_kernel(panel, group, n_leaf, n_levels, *refs):
    grams = refs[:n_leaf]
    lefts = refs[n_leaf : n_leaf + n_levels]
    rights = refs[n_leaf + n_levels : n_leaf + 2 * n_levels]
    solve_ref, tr_ref, m_ref, pick_ref = refs[n_leaf + 2 * n_levels :]
    p = m_ref.shape[1]
    own = lax.axis_index("grp")
    device = lax.axis_index("dev")
    for m in range(n_leaf):
        unpack_to(m_ref, jnp.bitwise_xor(own, m), grams[m][...])
    m_ref[4] = m_ref[0] + m_ref[1]
    m_ref[5] = m_ref[2] + m_ref[3]
    m_ref[6] = m_ref[4] + m_ref[5]
    pick_ref[0] = grams[0][...]
    pick_ref[1] = grams[1][...]
    for level in range(n_levels):

        @pl.when(device % 2 ** (level + 1) == 2**level - 1)
        def _(level=level):
            pick_ref[0] = lefts[level][...]
            pick_ref[1] = rights[level][...]

    unpack_to(m_ref, 7, pick_ref[0])
    unpack_to(m_ref, 8, pick_ref[1])
    m_ref[9] = m_ref[7] + m_ref[8]
    factor(m_ref, panel, group)
    ri = lax.broadcasted_iota(jnp.int32, (p, p), 0)
    ci = lax.broadcasted_iota(jnp.int32, (p, p), 1)

    def inverse(b):
        return jnp.concatenate(split(jnp.where(ci <= ri, m_ref[b], 0.0)), axis=0)

    def upper(b):
        whole = m_ref[b]
        return jnp.where(ci > ri, whole, jnp.where(ci == ri, 1.0 / whole, 0.0))

    for leaf in range(n_leaf):
        solve_ref[leaf] = inverse(leaf)
    keep = device != lax.axis_size("dev") - 1
    for q, (a, b, node) in enumerate(((0, 1, 4), (2, 3, 5), (4, 5, 6), (7, 8, 9))):
        made = applied(jnp.concatenate([upper(a), upper(b)], axis=0), inverse(node))
        tr_ref[q] = jnp.where(keep, made, 0.0) if q == 3 else made


def tree(grams, lefts, rights, group=4):
    p = grams[0].shape[1]
    panel = p // 4
    n_leaf = len(grams)
    arrays = [*grams, *lefts, *rights]
    return pl.pallas_call(
        functools.partial(tree_kernel, panel, group, n_leaf, len(lefts)),
        out_shape=(
            jax.ShapeDtypeStruct((n_leaf, 2 * p, p), bf16),
            jax.ShapeDtypeStruct((4, 2 * p, p), f32),
        ),
        in_specs=[VM] * len(arrays),
        out_specs=(VM, VM),
        scratch_shapes=[pltpu.VMEM((10, p, p), f32), pltpu.VMEM((2, *grams[0].shape), f32)],
        compiler_params=pltpu.CompilerParams(vmem_limit_bytes=16 << 20),
        cost_estimate=pl.CostEstimate(flops=0, bytes_accessed=24 << 20, transcendentals=0),
        name="tree",
    )(*arrays)


def basis_kernel(solve_ref, own_ref, near_ref, far_ref, basis_ref):
    own = lax.axis_index("grp")
    quarter = own_ref.shape[0]
    rows = (own_ref[...], near_ref[:quarter], far_ref[:quarter], far_ref[quarter:])
    for m, value in enumerate(rows):
        leaf = jnp.bitwise_xor(own, m)
        pair = jnp.concatenate(split(value), axis=0)
        dims = (((1,), (1,)), ((), ()))
        both = lax.dot_general(pair, solve_ref[leaf], dims, preferred_element_type=f32)
        both = both[:quarter] + both[quarter:]
        basis_ref[leaf] = both[:, : value.shape[1]] + both[:, value.shape[1] :]


def basis(solves, own, near, far):
    n_leaf = solves.shape[0]
    quarter, p = own.shape
    return pl.pallas_call(
        basis_kernel,
        out_shape=jax.ShapeDtypeStruct((n_leaf, quarter, p), f32),
        in_specs=[VM] * 4,
        out_specs=VM,
        compiler_params=pltpu.CompilerParams(vmem_limit_bytes=8 << 20),
        name="basis",
    )(solves, own, near, far)


def gathered(omega, dev_count):
    n_local = omega.shape[0]
    half = n_local // 2
    masks = [2**bit for bit in range(1, dev_count.bit_length() - 1)]
    waves = {}
    for order, first in ((masks, 0), (masks[::-1], half)):
        held = [(0, 0, omega[first : first + half])]
        for place, mask in enumerate(order):
            new = [
                (max(level, place) + (seen > 0), seen ^ mask, value) for level, seen, value in held
            ]
            for at, (level, seen, value) in enumerate(new):
                new[at] = (level, seen, swapped(value, "dev", mask))
            for level, seen, value in new:
                waves.setdefault(level, []).append((seen, first, value))
            held = held + new
    other = swapped(omega, "dev", 1)
    order = [mask * n_local + q for mask in (0, 1) for q in range(n_local)]
    groups = [[omega[:half], omega[half:], other]]
    for level in sorted(waves):
        wave = waves[level]
        for flip in (0, 1):
            for seen, first, value in wave:
                order.extend((seen ^ flip) * n_local + first + q for q in range(half))

        values = [value for _, _, value in wave]
        others = [swapped(value, "dev", 1) for value in values]
        if level == 0:
            groups.append(values + others)
        else:
            groups.extend([values, others])
    return groups, order


def on_device(omega, u_factor, v_factor, columns, ranks):
    n_local, n_blocks = u_factor.shape[1:3]
    leaf_rows, width = u_factor.shape[3:]
    dev_count = lax.axis_size("dev")
    grp_count = lax.axis_size("grp")
    assert n_local == grp_count == 4
    clusters = n_local * dev_count
    most = -(-11 * n_local * n_blocks // (10 * clusters))
    v = jnp.swapaxes(v_factor[0], 2, 3).reshape(n_local * n_blocks, width, leaf_rows)
    u = jnp.swapaxes(u_factor[0], 2, 3).reshape(n_local * n_blocks, width, leaf_rows)
    groups, order = gathered(omega[0], dev_count)
    depth = -(-most // 8) * 8
    unit = 2 * width
    columns = jnp.swapaxes(columns[0], 1, 2)
    slots, v = slot_table(tuple(order), columns, ranks[0], v, depth, unit, n_local)
    coeff = None
    start = 0
    for index, pieces in enumerate(groups):
        ahead = u if index == len(groups) - 4 else None
        coeff = coefficients(slots, v, pieces, start, most, unit, coeff, ahead)
        start += sum(piece.shape[0] for piece in pieces)
    made = {}
    for m in (3, 2, 1, 0):
        made[m] = sketch(coeff, u, m, n_blocks)
    across = swapped(made[3], "grp", 1)
    across = swapped(made[2] + across, "grp", 2)
    beside = swapped(made[1], "grp", 1)
    gram, rows_near, rows_far, rows_own = gram_of([made[0], beside, across], grp_count)
    near_in = swapped(gram, "grp", 1)
    far_in = swapped(gram, "grp", 2)
    pass_in = swapped(near_in, "grp", 2)
    rows_near = swapped(rows_near, "grp", 1)
    grams = [gram, near_in, far_in, pass_in]
    current = (gram + near_in) + (far_in + pass_in)
    lefts, rights = [], []
    masks = [2**bit for bit in range(dev_count.bit_length() - 1)]
    steps = [masks[:1]] + [masks[at : at + 2] for at in range(1, len(masks), 2)]
    for step in steps:
        first = swapped(current, "dev", step[0])
        wider = [swapped(current, "dev", extra ^ step[1]) for extra in (0, step[0])] if step[1:] else []
        lefts.append(current)
        rights.append(first)
        current = current + first
        if wider:
            lefts.append(current)
            rights.append(wider[0] + wider[1])
            current = current + rights[-1]
    quarter = rows_own.shape[0]
    rows_far = swapped(jnp.concatenate([rows_far, rows_near[quarter:]]), "grp", 2)
    solves, transfer = tree(grams, lefts, rights)
    return basis(solves, rows_own, rows_near, rows_far), transfer


def solution(mesh):
    placed = (
        P("grp", "dev", None, None),
        P("grp", "dev", None, None, None),
        P("grp", "dev", None, None, None),
        P("grp", "dev", None, None),
        P("grp", "dev", None),
    )
    return jax.shard_map(
        on_device,
        mesh=mesh,
        in_specs=placed,
        out_specs=(P("dev", "grp", None), P("dev", None, None)),
        check_vma=False,
    )
```
